512 devices in a mesh: seq: 16 (over z), head: 16 (over y, x), dp: 2 (over core).
Axes of the slice: x: 4, y: 4, z: 16, core: 2. Of those that a mesh axis runs over, the one named last changes fastest.
Arguments:
- local_qkv: bfloat16 [3, 32768, 2048], P(None, ('dp', 'seq'), 'head'), parts along dimension 1, may hold values from -150 to 150
- local_grad: bfloat16 [32768, 2048], P(('dp', 'seq'), 'head'), parts along dimension 0, may hold values from -5 to 5
- routed_qkv: bfloat16 [3, 32768, 2048], P(None, ('dp', 'seq'), 'head'), parts along dimension 1, may hold values from -150 to 150
- routed_grad: bfloat16 [32768, 2048], P(('dp', 'seq'), 'head'), parts along dimension 0, may hold values from -5 to 5
- cluster_ids: int32 [16, 32768], P('head', ('dp', 'seq')), parts along dimension 1, may hold values from 0 to 15, as said below
Outputs:
- local_out: bfloat16 [32768, 2048], P(('dp', 'seq'), 'head'), parts along dimension 0
- local_dqkv: bfloat16 [3, 32768, 2048], P(None, ('dp', 'seq'), 'head'), parts along dimension 1
- routed_out: bfloat16 [32768, 2048], P(('dp', 'seq'), 'head'), parts along dimension 0
- routed_dqkv: bfloat16 [3, 32768, 2048], P(None, ('dp', 'seq'), 'head'), parts along dimension 1
The draws below stay inside these ranges and needn't reach their ends.
There are 2 independent parts, one for each index of `dp`. The reference program is written for one: setup_inputs(seed, part) draws one part's arguments, and reference() takes and returns one part's arrays. A program takes and returns all parts, laid end to end along the dimension named above; each array names one. Nothing has to cross between parts.
Inputs may be any that keep to these rules, and one draw needn't show every extreme that they name: `cluster_ids`: for every clustered head each cluster holds exactly 1024 tokens, and at most 96 of the 1024 tokens of one index of seq lie in one cluster; some cluster reaches 96 in some index of seq.
All inputs are finite; a program needn't handle non-finite values.
Results may differ from the reference program's by a relative error of at most 0.024.
Values may be sent and summed in bfloat16 or wider, within the bound.
No kernel may reach another device: no remote copies, remote signals or barrier semaphores. Data moves between devices by JAX's collectives and lax.ppermute only.
A program may use at most 64 MiB of HBM per device.

```python
import jax
import jax.numpy as jnp
from jax import lax

HS = 128
TOK_DEV = 1024
WIN = 1024
HL = 16
HR = 16
LENGTH = 16384
NCLUST = 16
CSIZE = 1024


def signs_pair(key, total):
    shuffle = jax.random.permutation(key, total)
    primary = jnp.where(shuffle < total // 2, 1, -1).astype(jnp.int32)
    partner = jnp.where((shuffle >= total // 4) & (shuffle < 3 * total // 4), 1, -1).astype(jnp.int32)
    return (primary, partner)


def head_labels(key):
    seq_count = LENGTH // TOK_DEV
    per_source = CSIZE // seq_count
    weight_one = per_source // 8
    weight_two = per_source // 4
    split_keys = jax.random.split(key, 3)
    row_signs, row_twins = signs_pair(split_keys[0], NCLUST)
    col_signs, col_twins = signs_pair(split_keys[1], seq_count)
    counts = per_source + row_signs[:, None] * (weight_one * col_signs + weight_one * col_twins)[None, :] + weight_two * row_twins[:, None] * col_signs[None, :]
    bounds = jnp.cumsum(counts, axis=0)
    spots = jnp.arange(TOK_DEV, dtype=jnp.int32)
    label_grid = jnp.sum((spots[None, :, None] >= bounds.T[:, None, :]).astype(jnp.int32), axis=2)
    block_keys = jax.random.split(split_keys[2], seq_count)
    shuffles = jax.vmap(lambda block_key: jax.random.permutation(block_key, TOK_DEV))(block_keys)
    label_grid = jnp.take_along_axis(label_grid, shuffles, axis=1)
    return label_grid.reshape(LENGTH).astype(jnp.int32)


def all_labels(key):
    head_keys = jax.random.split(jax.random.fold_in(key, 11), HR)
    return jax.vmap(head_labels)(head_keys)


def base_values(key, shape):
    key_one = jax.random.fold_in(key, 0)
    return jnp.clip(jax.random.normal(key_one, shape, jnp.float32), -5.0, 5.0)


def draw_local_qkv(key, part):
    head_keys = jax.random.split(jax.random.fold_in(key, 5), HL)

    def one_head(head_key):
        key_one = jax.random.fold_in(head_key, 0)
        triple = base_values(key_one, (3, LENGTH, HS))
        return triple
    stacked = jax.vmap(one_head)(head_keys)
    return jnp.transpose(stacked, (1, 2, 0, 3)).reshape(3, LENGTH, HL * HS).astype(jnp.bfloat16)


def draw_routed_qkv(key, part):
    labels = all_labels(key)
    head_keys = jax.random.split(jax.random.fold_in(key, 17), HR)

    def one_head(head_key, labels_head):
        key_one = jax.random.fold_in(head_key, 0)
        triple = base_values(key_one, (3, LENGTH, HS))
        return triple
    stacked = jax.vmap(one_head)(head_keys, labels)
    return jnp.transpose(stacked, (1, 2, 0, 3)).reshape(3, LENGTH, HR * HS).astype(jnp.bfloat16)


def draw_cluster_ids(key, part):
    return all_labels(key).astype(jnp.int32)


def shard_levels(stream_key, extent, cuts, low, high):
    level, own = 1.0, jax.random.fold_in(stream_key, 6)
    for dim, shards_of in cuts:
        steps = jnp.exp(jax.random.uniform(jax.random.fold_in(own, dim), (shards_of,), jnp.float32, low / len(cuts), high / len(cuts)))
        level = level * jnp.repeat(steps, extent[dim] // shards_of).reshape([-1 if axis == dim else 1 for axis in range(len(extent))])
    return level


def bell_draw(key, shape, scale, bound, cuts=(), held_as=jnp.bfloat16):
    factor_of = shard_levels(key, shape, cuts, -0.22, 0.18) if cuts else 1.0
    array = jax.random.normal(key, shape, jnp.float32) * scale * factor_of
    return jnp.minimum(jnp.maximum(array, -bound), bound).astype(held_as)


def setup_inputs(seed: int = 0, part: int = 0) -> dict:
    streams_of = jax.random.split(jax.random.key(seed), 6)
    part_splits = jax.random.split(jax.random.fold_in(streams_of[5], part), 6)
    return {
        "local_qkv": draw_local_qkv(jax.random.fold_in(jax.random.fold_in(streams_of[5], part), 71), part),
        "local_grad": bell_draw(part_splits[1], (LENGTH, HL * HS), 1.0, 5.0, ((0, 16), (1, 16))),
        "routed_qkv": draw_routed_qkv(jax.random.fold_in(jax.random.fold_in(streams_of[5], part), 71), part),
        "routed_grad": bell_draw(part_splits[3], (LENGTH, HR * HS), 1.0, 5.0, ((0, 16), (1, 16))),
        "cluster_ids": draw_cluster_ids(jax.random.fold_in(jax.random.fold_in(streams_of[5], part), 71), part),
    }


masked_fill = -1.0e30


def attend_rows(query_rows, grad_rows, key_rows, value_rows, allowed):
    factor = query_rows.shape[-1] ** -0.5
    scores = jnp.dot(query_rows, key_rows.T, preferred_element_type=jnp.float32) * factor
    scores = jnp.where(allowed, scores, masked_fill)
    row_peak = jnp.max(scores, axis=1, keepdims=True)
    exp_scores = jnp.exp(scores - row_peak)
    row_total = jnp.sum(exp_scores, axis=1, keepdims=True)
    row_probs = exp_scores / row_total
    weights = row_probs.astype(jnp.bfloat16)
    output = jnp.dot(weights, value_rows, preferred_element_type=jnp.float32).astype(jnp.bfloat16)
    output = lax.optimization_barrier(output)
    row_delta = jnp.sum(grad_rows.astype(jnp.float32) * output.astype(jnp.float32), axis=1)
    dprobs = jnp.dot(grad_rows, value_rows.T, preferred_element_type=jnp.float32)
    dscore = (row_probs * (dprobs - row_delta[:, None])).astype(jnp.bfloat16)
    dquery = (jnp.dot(dscore, key_rows, preferred_element_type=jnp.float32) * factor).astype(jnp.bfloat16)
    key_grad = jnp.dot(dscore.T, query_rows, preferred_element_type=jnp.float32) * factor
    dvalue = jnp.dot(weights.T, grad_rows, preferred_element_type=jnp.float32)
    return output, dquery, key_grad, dvalue


def local_head(head_qkv, head_grad):
    block_rows = min(TOK_DEV, 512)
    key_span = WIN + block_rows
    head_size = head_qkv.shape[-1]
    zeros_pad = jnp.zeros((WIN, head_size), head_qkv.dtype)
    padded_keys = jnp.concatenate([zeros_pad, head_qkv[1]], axis=0)
    padded_values = jnp.concatenate([zeros_pad, head_qkv[2]], axis=0)

    def block_step(carried, block_index):
        key_acc, value_acc = carried
        row_start = block_index * block_rows
        query_block = lax.dynamic_slice_in_dim(head_qkv[0], row_start, block_rows, 0)
        grad_block = lax.dynamic_slice_in_dim(head_grad, row_start, block_rows, 0)
        key_window = lax.dynamic_slice_in_dim(padded_keys, row_start, key_span, 0)
        value_window = lax.dynamic_slice_in_dim(padded_values, row_start, key_span, 0)
        relative = row_start - WIN + jnp.arange(key_span, dtype=jnp.int32)
        query_pos = row_start + jnp.arange(block_rows, dtype=jnp.int32)
        allowed = (relative[None, :] <= query_pos[:, None]) & (relative[None, :] > query_pos[:, None] - WIN) & (relative >= 0)[None, :]
        output, dquery, key_grad, dvalue = attend_rows(query_block, grad_block, key_window, value_window, allowed)
        key_acc = lax.dynamic_update_slice_in_dim(key_acc, lax.dynamic_slice_in_dim(key_acc, row_start, key_span, 0) + key_grad, row_start, 0)
        value_acc = lax.dynamic_update_slice_in_dim(value_acc, lax.dynamic_slice_in_dim(value_acc, row_start, key_span, 0) + dvalue, row_start, 0)
        return (key_acc, value_acc), (output, dquery)

    initial = (jnp.zeros((LENGTH + WIN, head_size), jnp.float32), jnp.zeros((LENGTH + WIN, head_size), jnp.float32))
    (key_acc, value_acc), (outputs, dqueries) = lax.scan(block_step, initial, jnp.arange(LENGTH // block_rows, dtype=jnp.int32))
    result = outputs.reshape(LENGTH, head_size)
    gradients = jnp.stack([dqueries.reshape(LENGTH, head_size), key_acc[WIN:].astype(jnp.bfloat16), value_acc[WIN:].astype(jnp.bfloat16)])
    return result, gradients


def cluster_pass(packed):
    member_count = packed.shape[0]
    allowed = jnp.ones((member_count, member_count), dtype=bool)
    output, dquery, key_grad, dvalue = attend_rows(packed[:, 0], packed[:, 3], packed[:, 1], packed[:, 2], allowed)
    return jnp.stack([output, dquery, key_grad.astype(jnp.bfloat16), dvalue.astype(jnp.bfloat16)], axis=1)


def routed_head(head_qkv, head_grad, labels):
    grouping = jnp.argsort(labels, stable=True).astype(jnp.int32).reshape(NCLUST, CSIZE)
    payload = jnp.stack([head_qkv[0], head_qkv[1], head_qkv[2], head_grad], axis=1)
    grouped = payload[grouping]
    results = lax.map(cluster_pass, grouped)
    arranged = jnp.zeros_like(payload).at[grouping.reshape(-1)].set(results.reshape(LENGTH, 4, HS))
    return arranged[:, 0], jnp.transpose(arranged[:, 1:], (1, 0, 2))


def reference(local_qkv, local_grad, routed_qkv, routed_grad, cluster_ids):
    local_heads = jnp.transpose(local_qkv.reshape(3, LENGTH, HL, HS), (2, 0, 1, 3))
    local_grads = jnp.transpose(local_grad.reshape(LENGTH, HL, HS), (1, 0, 2))
    local_out, local_dqkv = lax.map(lambda packed: local_head(packed[0], packed[1]), (local_heads, local_grads))
    local_out = jnp.transpose(local_out, (1, 0, 2)).reshape(LENGTH, HL * HS)
    local_dqkv = jnp.transpose(local_dqkv, (1, 2, 0, 3)).reshape(3, LENGTH, HL * HS)
    routed_heads = jnp.transpose(routed_qkv.reshape(3, LENGTH, HR, HS), (2, 0, 1, 3))
    routed_grads = jnp.transpose(routed_grad.reshape(LENGTH, HR, HS), (1, 0, 2))
    routed_out, routed_dqkv = lax.map(lambda packed: routed_head(packed[0], packed[1], packed[2]), (routed_heads, routed_grads, cluster_ids))
    routed_out = jnp.transpose(routed_out, (1, 0, 2)).reshape(LENGTH, HR * HS)
    routed_dqkv = jnp.transpose(routed_dqkv, (1, 2, 0, 3)).reshape(3, LENGTH, HR * HS)
    return local_out, local_dqkv, routed_out, routed_dqkv
```

```python
import jax
import jax.numpy as jnp
from jax import lax
from jax.experimental import pallas as pl
from jax.experimental.pallas import tpu as pltpu
from jax.sharding import PartitionSpec as P

WIN = 1024
SLOTS = 96
EMPTY = 512.0
masked_fill = -1e30


def dot_nn(a, b):
    return lax.dot_general(a, b, (((1,), (0,)), ((), ())), preferred_element_type=jnp.float32)


def dot_nt(a, b):
    return lax.dot_general(a, b, (((1,), (1,)), ((), ())), preferred_element_type=jnp.float32)


def dot_tn(a, b):
    return lax.dot_general(a, b, (((0,), (0,)), ((), ())), preferred_element_type=jnp.float32)


def softmax_grad(query, key, value, grad, factor, mask):
    scores = dot_nt(query, key)
    if mask is not None:
        scores = mask(scores)
    peak = jnp.max(scores, axis=1, keepdims=True)
    probs = jnp.exp((scores - peak) * factor)
    probs = probs * (1.0 / jnp.sum(probs, axis=1, keepdims=True))
    weights = probs.astype(jnp.bfloat16)
    output = dot_nn(weights, value).astype(jnp.bfloat16)
    delta = jnp.sum(
        grad.astype(jnp.float32) * output.astype(jnp.float32), axis=1, keepdims=True
    )
    dscores = (probs * (dot_nt(grad, value) - delta)).astype(jnp.bfloat16)
    dquery = (dot_nn(dscores, key) * factor).astype(jnp.bfloat16)
    return output, dquery, dscores, weights


def route_kernel(labels_ref, qkv_ref, grad_ref, buffer_ref, target_ref):
    tokens = labels_ref.shape[1]
    clusters = buffer_ref.shape[0]
    labels = labels_ref[...]
    block = 256
    lower = lax.broadcasted_iota(jnp.int32, (block, block), 0)
    upper = lax.broadcasted_iota(jnp.int32, (block, block), 1)
    triangle = (lower <= upper).astype(jnp.bfloat16)
    cluster_rows = lax.broadcasted_iota(jnp.int32, (clusters, block), 0)
    running = jnp.zeros((clusters, 1), jnp.float32)
    targets = []
    for start in range(0, tokens, block):
        part = labels[:, start : start + block]
        onehot = (cluster_rows == part).astype(jnp.float32)
        within = dot_nn(onehot.astype(jnp.bfloat16), triangle) + running
        rank = jnp.sum(within * onehot, axis=0, keepdims=True).astype(jnp.int32) - 1
        targets.append(part * SLOTS + rank)
        running = running + jnp.sum(onehot, axis=1, keepdims=True)
    target = jnp.concatenate(targets, axis=1)
    target_ref[...] = jnp.transpose(
        jnp.broadcast_to(target.astype(jnp.float32), (128, tokens))
    ).astype(jnp.int32)
    payload = jnp.concatenate([qkv_ref[0], qkv_ref[1], qkv_ref[2], grad_ref[...]], axis=1)
    head_size = grad_ref.shape[1]
    slot_rows = lax.broadcasted_iota(jnp.int32, (SLOTS, tokens), 0)
    fill_rows = lax.broadcasted_iota(jnp.int32, (SLOTS, head_size), 0)
    for cluster in range(clusters):
        select = (slot_rows + cluster * SLOTS == target).astype(jnp.float32).astype(jnp.bfloat16)
        rows = dot_nn(select, payload)
        count = running[cluster : cluster + 1, :].astype(jnp.int32)
        first = jnp.where(fill_rows < count, rows[:, :head_size], EMPTY)
        buffer_ref[cluster, :, :head_size] = first.astype(jnp.bfloat16)
        buffer_ref[cluster, :, head_size:] = rows[:, head_size:].astype(jnp.bfloat16)


def route(labels, qkv, grad, clusters):
    tokens, head_size = grad.shape
    return pl.pallas_call(
        route_kernel,
        out_shape=(
            jax.ShapeDtypeStruct((clusters, SLOTS, 4 * head_size), jnp.bfloat16),
            jax.ShapeDtypeStruct((tokens, 128), jnp.int32),
        ),
        compiler_params=pltpu.CompilerParams(vmem_limit_bytes=48 << 20),
        name="route",
    )(labels, qkv, grad)


def cluster_kernel(received_ref, result_ref, counts_vmem, counts_smem, rows_ref, out_ref, sem):
    sources = received_ref.shape[0]
    head_size = received_ref.shape[2] // 4
    tokens = rows_ref.shape[1] - SLOTS
    factor = head_size ** (-0.5)
    filled = []
    for source in range(sources):
        mark = received_ref[source, :, :head_size].astype(jnp.float32)
        filled.append(jnp.sum((mark < EMPTY).astype(jnp.float32), axis=0, keepdims=True))
    counts_vmem[...] = jnp.concatenate(filled, axis=0).astype(jnp.int32)
    copy = pltpu.make_async_copy(counts_vmem, counts_smem, sem)
    copy.start()
    copy.wait()
    starts = []
    start = 0
    for source in range(sources):
        starts.append(start)
        for part in range(4):
            lanes = slice(part * head_size, (part + 1) * head_size)
            rows_ref[part, pl.ds(start, SLOTS), :] = received_ref[source, :, lanes].astype(
                jnp.float32
            )
        start = jnp.minimum(start + counts_smem[source, 0], tokens)
    block = 256
    key = rows_ref[1, :tokens, :].astype(jnp.bfloat16)
    value = rows_ref[2, :tokens, :].astype(jnp.bfloat16)
    key_grad = jnp.zeros((tokens, head_size), jnp.float32)
    value_grad = jnp.zeros((tokens, head_size), jnp.float32)
    for row in range(0, tokens, block):
        query = rows_ref[0, row : row + block, :].astype(jnp.bfloat16)
        grad = rows_ref[3, row : row + block, :].astype(jnp.bfloat16)
        output, dquery, dscores, weights = softmax_grad(query, key, value, grad, factor, None)
        out_ref[0, row : row + block, :] = output.astype(jnp.float32)
        out_ref[1, row : row + block, :] = dquery.astype(jnp.float32)
        key_grad = key_grad + dot_tn(dscores, query)
        value_grad = value_grad + dot_tn(weights, grad)
    out_ref[2, :tokens, :] = key_grad * factor
    out_ref[3, :tokens, :] = value_grad
    out_ref[:, tokens:, :] = jnp.zeros((4, SLOTS, head_size), jnp.float32)
    for source in range(sources):
        for part in range(4):
            lanes = slice(part * head_size, (part + 1) * head_size)
            result_ref[source, :, lanes] = out_ref[part, pl.ds(starts[source], SLOTS), :].astype(
                jnp.bfloat16
            )


def cluster_attention(received, tokens):
    sources, slots, width = received.shape
    return pl.pallas_call(
        cluster_kernel,
        out_shape=jax.ShapeDtypeStruct(received.shape, jnp.bfloat16),
        scratch_shapes=[
            pltpu.VMEM((sources, 128), jnp.int32),
            pltpu.SMEM((sources, 128), jnp.int32),
            pltpu.VMEM((4, tokens + SLOTS, width // 4), jnp.float32),
            pltpu.VMEM((4, tokens + SLOTS, width // 4), jnp.float32),
            pltpu.SemaphoreType.DMA,
        ],
        compiler_params=pltpu.CompilerParams(vmem_limit_bytes=56 << 20),
        name="cluster",
    )(received)


def unroute_kernel(returned_ref, target_ref, output_ref, grads_ref):
    clusters = returned_ref.shape[0]
    tokens, head_size = output_ref.shape
    slots = clusters * SLOTS
    rows = returned_ref[...].reshape(slots, 4 * head_size)
    block = 256
    lanes = lax.broadcasted_iota(jnp.int32, (block, 128), 1)
    for row in range(0, tokens, block):
        target = target_ref[row : row + block, :]
        select = jnp.concatenate(
            [
                (lanes + lane == target).astype(jnp.float32).astype(jnp.bfloat16)
                for lane in range(0, slots, 128)
            ],
            axis=1,
        )
        picked = dot_nn(select, rows).astype(jnp.bfloat16)
        output_ref[row : row + block, :] = picked[:, :head_size]
        for part in range(3):
            grads_ref[part, row : row + block, :] = picked[
                :, (part + 1) * head_size : (part + 2) * head_size
            ]


def unroute(returned, target, head_size):
    tokens = target.shape[0]
    return pl.pallas_call(
        unroute_kernel,
        out_shape=(
            jax.ShapeDtypeStruct((tokens, head_size), jnp.bfloat16),
            jax.ShapeDtypeStruct((3, tokens, head_size), jnp.bfloat16),
        ),
        compiler_params=pltpu.CompilerParams(vmem_limit_bytes=48 << 20),
        name="unroute",
    )(returned, target)


def local_kernel(
    index_ref, qkv_ref, grad_ref, prev_ref, output_ref, dquery_ref, own_ref, late_ref, keys, values, key_acc, value_acc
):
    tokens, head_size = grad_ref.shape
    factor = head_size ** (-0.5)
    block = 256
    span = WIN + block
    keys[:tokens, :] = prev_ref[0]
    keys[tokens:, :] = qkv_ref[1]
    values[:tokens, :] = prev_ref[1]
    values[tokens:, :] = qkv_ref[2]
    key_acc[...] = jnp.zeros_like(key_acc)
    value_acc[...] = jnp.zeros_like(value_acc)
    rows = lax.broadcasted_iota(jnp.int32, (block, block), 0)
    columns = lax.broadcasted_iota(jnp.int32, (block, block), 1)
    whole = lax.broadcasted_iota(jnp.int32, (block, span), 1)
    first_key = jnp.where(index_ref[0] == 0, tokens, 0)

    for row in range(0, tokens, block):

        def mask(scores, row=row):
            head = jnp.where(columns > rows, scores[:, :block], masked_fill)
            tail = jnp.where(columns <= rows, scores[:, span - block :], masked_fill)
            joined = jnp.concatenate([head, scores[:, block : span - block], tail], axis=1)
            return jnp.where(whole + row >= first_key, joined, masked_fill)

        query = qkv_ref[0, row : row + block, :]
        grad = grad_ref[row : row + block, :]
        key = keys[row : row + span, :]
        value = values[row : row + span, :]
        output, dquery, dscores, weights = softmax_grad(query, key, value, grad, factor, mask)
        output_ref[row : row + block, :] = output
        dquery_ref[row : row + block, :] = dquery
        key_acc[row : row + span, :] += dot_tn(dscores, query)
        value_acc[row : row + span, :] += dot_tn(weights, grad)
    late_ref[0] = (key_acc[:tokens, :] * factor).astype(jnp.bfloat16)
    late_ref[1] = value_acc[:tokens, :].astype(jnp.bfloat16)
    own_ref[0] = key_acc[tokens:, :] * factor
    own_ref[1] = value_acc[tokens:, :]


def local_attention(index, qkv, grad, prev):
    tokens, head_size = grad.shape
    vmem = pl.BlockSpec(memory_space=pltpu.VMEM)
    return pl.pallas_call(
        local_kernel,
        out_shape=(
            jax.ShapeDtypeStruct((tokens, head_size), jnp.bfloat16),
            jax.ShapeDtypeStruct((tokens, head_size), jnp.bfloat16),
            jax.ShapeDtypeStruct((2, tokens, head_size), jnp.float32),
            jax.ShapeDtypeStruct((2, tokens, head_size), jnp.bfloat16),
        ),
        in_specs=[pl.BlockSpec(memory_space=pltpu.SMEM), vmem, vmem, vmem],
        scratch_shapes=[
            pltpu.VMEM((2 * tokens, head_size), jnp.bfloat16),
            pltpu.VMEM((2 * tokens, head_size), jnp.bfloat16),
            pltpu.VMEM((2 * tokens, head_size), jnp.float32),
            pltpu.VMEM((2 * tokens, head_size), jnp.float32),
        ],
        compiler_params=pltpu.CompilerParams(vmem_limit_bytes=56 << 20),
        name="local",
    )(index, qkv, grad, prev)


def shifted(block, distance):
    devices = range(lax.axis_size("seq"))
    return lax.ppermute(
        block, "seq", [(i - distance, i) for i in devices if i - distance in devices]
    )


def on_device(local_qkv, local_grad, routed_qkv, routed_grad, cluster_ids):
    tokens, head_size = local_grad.shape
    clusters = lax.axis_size("seq")
    prev = shifted(local_qkv[1:], 1)
    buffer, target = route(cluster_ids, routed_qkv, routed_grad, clusters)
    received = lax.all_to_all(buffer, "seq", split_axis=0, concat_axis=0, tiled=True)
    index = lax.axis_index("seq").astype(jnp.int32).reshape(1)
    local_out, dquery, own, late = local_attention(index, local_qkv, local_grad, prev)
    late = shifted(late, -1)
    returned = lax.all_to_all(
        cluster_attention(received, tokens), "seq", split_axis=0, concat_axis=0, tiled=True
    )
    joined = (own + late.astype(jnp.float32)).astype(jnp.bfloat16)
    local_dqkv = jnp.concatenate([dquery[None], joined], axis=0)
    routed_out, routed_dqkv = unroute(returned, target, head_size)
    return (local_out, local_dqkv, routed_out, routed_dqkv)


def solution(mesh):
    rows = P(("dp", "seq"), "head")
    stacked = P(None, ("dp", "seq"), "head")
    return jax.shard_map(
        on_device,
        mesh=mesh,
        in_specs=(stacked, rows, stacked, rows, P("head", ("dp", "seq"))),
        out_specs=(rows, stacked, rows, stacked),
        check_vma=False,
    )
```

```python
import jax
import jax.numpy as jnp
from jax import lax
from jax.experimental import pallas as pl
from jax.experimental.pallas import tpu as pltpu
from jax.sharding import PartitionSpec as P

WIN = 1024
SLOTS = 96
EMPTY = 512.0
masked_fill = -1e30


def dot_nn(a, b):
    return lax.dot_general(a, b, (((1,), (0,)), ((), ())), preferred_element_type=jnp.float32)


def dot_nt(a, b):
    return lax.dot_general(a, b, (((1,), (1,)), ((), ())), preferred_element_type=jnp.float32)


def dot_tn(a, b):
    return lax.dot_general(a, b, (((0,), (0,)), ((), ())), preferred_element_type=jnp.float32)


def softmax_grad(query, key, value, grad, factor, mask):
    scores = dot_nt(query, key)
    if mask is not None:
        scores = mask(scores)
    peak = jnp.max(scores, axis=1, keepdims=True)
    probs = jnp.exp((scores - peak) * factor)
    probs = probs * (1.0 / jnp.sum(probs, axis=1, keepdims=True))
    weights = probs.astype(jnp.bfloat16)
    output = dot_nn(weights, value).astype(jnp.bfloat16)
    delta = jnp.sum(
        grad.astype(jnp.float32) * output.astype(jnp.float32), axis=1, keepdims=True
    )
    dscores = (probs * (dot_nt(grad, value) - delta)).astype(jnp.bfloat16)
    dquery = (dot_nn(dscores, key) * factor).astype(jnp.bfloat16)
    return output, dquery, dscores, weights


def route_kernel(labels_ref, qkv_ref, grad_ref, buffer_ref, target_ref):
    tokens = labels_ref.shape[1]
    clusters = buffer_ref.shape[0]
    labels = labels_ref[...]
    block = 256
    lower = lax.broadcasted_iota(jnp.int32, (block, block), 0)
    upper = lax.broadcasted_iota(jnp.int32, (block, block), 1)
    triangle = (lower <= upper).astype(jnp.bfloat16)
    cluster_rows = lax.broadcasted_iota(jnp.int32, (clusters, block), 0)
    running = jnp.zeros((clusters, 1), jnp.float32)
    targets = []
    for start in range(0, tokens, block):
        part = labels[:, start : start + block]
        onehot = (cluster_rows == part).astype(jnp.float32)
        within = dot_nn(onehot.astype(jnp.bfloat16), triangle) + running
        rank = jnp.sum(within * onehot, axis=0, keepdims=True).astype(jnp.int32) - 1
        targets.append(part * SLOTS + rank)
        running = running + jnp.sum(onehot, axis=1, keepdims=True)
    target = jnp.concatenate(targets, axis=1)
    target_ref[...] = jnp.transpose(
        jnp.broadcast_to(target.astype(jnp.float32), (128, tokens))
    ).astype(jnp.int32)
    payload = jnp.concatenate([qkv_ref[0], qkv_ref[1], qkv_ref[2], grad_ref[...]], axis=1)
    head_size = grad_ref.shape[1]
    slot_rows = lax.broadcasted_iota(jnp.int32, (SLOTS, tokens), 0)
    fill_rows = lax.broadcasted_iota(jnp.int32, (SLOTS, head_size), 0)
    for cluster in range(clusters):
        select = (slot_rows + cluster * SLOTS == target).astype(jnp.float32).astype(jnp.bfloat16)
        rows = dot_nn(select, payload)
        count = running[cluster : cluster + 1, :].astype(jnp.int32)
        first = jnp.where(fill_rows < count, rows[:, :head_size], EMPTY)
        buffer_ref[cluster, :, :head_size] = first.astype(jnp.bfloat16)
        buffer_ref[cluster, :, head_size:] = rows[:, head_size:].astype(jnp.bfloat16)


def route(labels, qkv, grad, clusters):
    tokens, head_size = grad.shape
    return pl.pallas_call(
        route_kernel,
        out_shape=(
            jax.ShapeDtypeStruct((clusters, SLOTS, 4 * head_size), jnp.bfloat16),
            jax.ShapeDtypeStruct((tokens, 128), jnp.int32),
        ),
        compiler_params=pltpu.CompilerParams(vmem_limit_bytes=20 << 20),
        name="route",
    )(labels, qkv, grad)


def cluster_kernel(received_ref, result_ref, counts_vmem, counts_smem, rows_ref, out_ref, sem):
    sources = received_ref.shape[0]
    head_size = received_ref.shape[2] // 4
    tokens = rows_ref.shape[1] - SLOTS
    factor = head_size ** (-0.5)
    filled = []
    for source in range(sources):
        mark = received_ref[source, :, :head_size].astype(jnp.float32)
        filled.append(jnp.sum((mark < EMPTY).astype(jnp.float32), axis=0, keepdims=True))
    counts_vmem[...] = jnp.concatenate(filled, axis=0).astype(jnp.int32)
    copy = pltpu.make_async_copy(counts_vmem, counts_smem, sem)
    copy.start()
    copy.wait()
    starts = []
    start = 0
    for source in range(sources):
        starts.append(start)
        for part in range(4):
            lanes = slice(part * head_size, (part + 1) * head_size)
            rows_ref[part, pl.ds(start, SLOTS), :] = received_ref[source, :, lanes].astype(
                jnp.float32
            )
        start = jnp.minimum(start + counts_smem[source, 0], tokens)
    block = 256
    key = rows_ref[1, :tokens, :].astype(jnp.bfloat16)
    value = rows_ref[2, :tokens, :].astype(jnp.bfloat16)
    key_grad = jnp.zeros((tokens, head_size), jnp.float32)
    value_grad = jnp.zeros((tokens, head_size), jnp.float32)
    for row in range(0, tokens, block):
        query = rows_ref[0, row : row + block, :].astype(jnp.bfloat16)
        grad = rows_ref[3, row : row + block, :].astype(jnp.bfloat16)
        output, dquery, dscores, weights = softmax_grad(query, key, value, grad, factor, None)
        out_ref[0, row : row + block, :] = output.astype(jnp.float32)
        out_ref[1, row : row + block, :] = dquery.astype(jnp.float32)
        key_grad = key_grad + dot_tn(dscores, query)
        value_grad = value_grad + dot_tn(weights, grad)
    out_ref[2, :tokens, :] = key_grad * factor
    out_ref[3, :tokens, :] = value_grad
    out_ref[:, tokens:, :] = jnp.zeros((4, SLOTS, head_size), jnp.float32)
    for source in range(sources):
        for part in range(4):
            lanes = slice(part * head_size, (part + 1) * head_size)
            result_ref[source, :, lanes] = out_ref[part, pl.ds(starts[source], SLOTS), :].astype(
                jnp.bfloat16
            )


def cluster_attention(received, tokens):
    sources, slots, width = received.shape
    vmem = pl.BlockSpec(memory_space=pltpu.VMEM)
    return pl.pallas_call(
        cluster_kernel,
        out_shape=jax.ShapeDtypeStruct(received.shape, jnp.bfloat16),
        in_specs=[vmem],
        out_specs=vmem,
        scratch_shapes=[
            pltpu.VMEM((sources, 128), jnp.int32),
            pltpu.SMEM((sources, 128), jnp.int32),
            pltpu.VMEM((4, tokens + SLOTS, width // 4), jnp.float32),
            pltpu.VMEM((4, tokens + SLOTS, width // 4), jnp.float32),
            pltpu.SemaphoreType.DMA,
        ],
        compiler_params=pltpu.CompilerParams(vmem_limit_bytes=28 << 20),
        name="cluster",
    )(received)


def unroute_kernel(returned_ref, target_ref, output_ref, grads_ref):
    clusters = returned_ref.shape[0]
    tokens, head_size = output_ref.shape
    slots = clusters * SLOTS
    rows = returned_ref[...].reshape(slots, 4 * head_size)
    block = 256
    lanes = lax.broadcasted_iota(jnp.int32, (block, 128), 1)
    for row in range(0, tokens, block):
        target = target_ref[row : row + block, :]
        select = jnp.concatenate(
            [
                (lanes + lane == target).astype(jnp.float32).astype(jnp.bfloat16)
                for lane in range(0, slots, 128)
            ],
            axis=1,
        )
        picked = dot_nn(select, rows).astype(jnp.bfloat16)
        output_ref[row : row + block, :] = picked[:, :head_size]
        for part in range(3):
            grads_ref[part, row : row + block, :] = picked[
                :, (part + 1) * head_size : (part + 2) * head_size
            ]


def unroute(returned, target, head_size):
    tokens = target.shape[0]
    return pl.pallas_call(
        unroute_kernel,
        out_shape=(
            jax.ShapeDtypeStruct((tokens, head_size), jnp.bfloat16),
            jax.ShapeDtypeStruct((3, tokens, head_size), jnp.bfloat16),
        ),
        in_specs=[pl.BlockSpec(memory_space=pltpu.VMEM)] * 2,
        compiler_params=pltpu.CompilerParams(vmem_limit_bytes=20 << 20),
        name="unroute",
    )(returned, target)


def local_kernel(
    index_ref, qkv_ref, grad_ref, prev_ref, output_ref, dquery_ref, own_ref, late_ref, keys, values, key_acc, value_acc
):
    tokens, head_size = grad_ref.shape
    factor = head_size ** (-0.5)
    block = 256
    span = WIN + block
    keys[:tokens, :] = prev_ref[0]
    keys[tokens:, :] = qkv_ref[1]
    values[:tokens, :] = prev_ref[1]
    values[tokens:, :] = qkv_ref[2]
    key_acc[...] = jnp.zeros_like(key_acc)
    value_acc[...] = jnp.zeros_like(value_acc)
    rows = lax.broadcasted_iota(jnp.int32, (block, block), 0)
    columns = lax.broadcasted_iota(jnp.int32, (block, block), 1)
    whole = lax.broadcasted_iota(jnp.int32, (block, span), 1)
    first_key = jnp.where(index_ref[0] == 0, tokens, 0)

    for row in range(0, tokens, block):

        def mask(scores, row=row):
            head = jnp.where(columns > rows, scores[:, :block], masked_fill)
            tail = jnp.where(columns <= rows, scores[:, span - block :], masked_fill)
            joined = jnp.concatenate([head, scores[:, block : span - block], tail], axis=1)
            return jnp.where(whole + row >= first_key, joined, masked_fill)

        query = qkv_ref[0, row : row + block, :]
        grad = grad_ref[row : row + block, :]
        key = keys[row : row + span, :]
        value = values[row : row + span, :]
        output, dquery, dscores, weights = softmax_grad(query, key, value, grad, factor, mask)
        output_ref[row : row + block, :] = output
        dquery_ref[row : row + block, :] = dquery
        key_acc[row : row + span, :] += dot_tn(dscores, query)
        value_acc[row : row + span, :] += dot_tn(weights, grad)
    late_ref[0] = (key_acc[:tokens, :] * factor).astype(jnp.bfloat16)
    late_ref[1] = value_acc[:tokens, :].astype(jnp.bfloat16)
    own_ref[0] = key_acc[tokens:, :] * factor
    own_ref[1] = value_acc[tokens:, :]


def local_attention(index, qkv, grad, prev):
    tokens, head_size = grad.shape
    vmem = pl.BlockSpec(memory_space=pltpu.VMEM)
    return pl.pallas_call(
        local_kernel,
        out_shape=(
            jax.ShapeDtypeStruct((tokens, head_size), jnp.bfloat16),
            jax.ShapeDtypeStruct((tokens, head_size), jnp.bfloat16),
            jax.ShapeDtypeStruct((2, tokens, head_size), jnp.float32),
            jax.ShapeDtypeStruct((2, tokens, head_size), jnp.bfloat16),
        ),
        in_specs=[pl.BlockSpec(memory_space=pltpu.SMEM), vmem, vmem, vmem],
        scratch_shapes=[
            pltpu.VMEM((2 * tokens, head_size), jnp.bfloat16),
            pltpu.VMEM((2 * tokens, head_size), jnp.bfloat16),
            pltpu.VMEM((2 * tokens, head_size), jnp.float32),
            pltpu.VMEM((2 * tokens, head_size), jnp.float32),
        ],
        compiler_params=pltpu.CompilerParams(vmem_limit_bytes=28 << 20),
        name="local",
    )(index, qkv, grad, prev)


def shifted(block, distance):
    devices = range(lax.axis_size("seq"))
    return lax.ppermute(
        block, "seq", [(i - distance, i) for i in devices if i - distance in devices]
    )


def exchange(block):
    return lax.all_to_all(block, "seq", split_axis=0, concat_axis=0, tiled=True)


def routed_first(local_qkv, local_grad, routed_qkv, routed_grad, cluster_ids):
    tokens, head_size = local_grad.shape
    buffer, target = route(cluster_ids, routed_qkv, routed_grad, lax.axis_size("seq"))
    received = exchange(buffer)
    halo, buffer = lax.optimization_barrier((local_qkv[1:], buffer))
    prev = shifted(halo, 1)
    result = cluster_attention(received, tokens)
    result, prev = lax.optimization_barrier((result, prev))
    returned = exchange(result)
    index = lax.axis_index("seq").astype(jnp.int32).reshape(1)
    local_out, dquery, own, late = local_attention(index, local_qkv, local_grad, prev)
    late = shifted(late, -1)
    joined = (own + late.astype(jnp.float32)).astype(jnp.bfloat16)
    local_dqkv = jnp.concatenate([dquery[None], joined], axis=0)
    routed_out, routed_dqkv = unroute(returned, target, head_size)
    return (local_out, local_dqkv, routed_out, routed_dqkv)


def local_first(local_qkv, local_grad, routed_qkv, routed_grad, cluster_ids):
    tokens, head_size = local_grad.shape
    prev = shifted(local_qkv[1:], 1)
    buffer, target = route(cluster_ids, routed_qkv, routed_grad, lax.axis_size("seq"))
    index = lax.axis_index("seq").astype(jnp.int32).reshape(1)
    local_out, dquery, own, late = local_attention(index, local_qkv, local_grad, prev)
    buffer, late = lax.optimization_barrier((buffer, late))
    received = exchange(buffer)
    late = shifted(late, -1)
    result = cluster_attention(received, tokens)
    result, late = lax.optimization_barrier((result, late))
    returned = exchange(result)
    joined = (own + late.astype(jnp.float32)).astype(jnp.bfloat16)
    local_dqkv = jnp.concatenate([dquery[None], joined], axis=0)
    routed_out, routed_dqkv = unroute(returned, target, head_size)
    return (local_out, local_dqkv, routed_out, routed_dqkv)


def on_device(*arrays):
    return lax.cond(lax.axis_index("dp") == 0, routed_first, local_first, *arrays)


def solution(mesh):
    rows = P(("dp", "seq"), "head")
    stacked = P(None, ("dp", "seq"), "head")
    return jax.shard_map(
        on_device,
        mesh=mesh,
        in_specs=(stacked, rows, stacked, rows, P("head", ("dp", "seq"))),
        out_specs=(rows, stacked, rows, stacked),
        check_vma=False,
    )
```

```python
import jax
import jax.numpy as jnp
from jax import lax
from jax.experimental import pallas as pl
from jax.experimental.pallas import tpu as pltpu
from jax.sharding import PartitionSpec as P

WIN = 1024
SLOTS = 96
EMPTY = 512.0
masked_fill = -1e30


def dot_nn(a, b):
    return lax.dot_general(a, b, (((1,), (0,)), ((), ())), preferred_element_type=jnp.float32)


def dot_nt(a, b):
    return lax.dot_general(a, b, (((1,), (1,)), ((), ())), preferred_element_type=jnp.float32)


def dot_tn(a, b):
    return lax.dot_general(a, b, (((0,), (0,)), ((), ())), preferred_element_type=jnp.float32)


def softmax_grad(query, key, value, grad, factor, mask):
    scores = dot_nt(query, key)
    if mask is not None:
        scores = mask(scores)
    peak = jnp.max(scores, axis=1, keepdims=True)
    probs = jnp.exp((scores - peak) * factor)
    probs = probs * (1.0 / jnp.sum(probs, axis=1, keepdims=True))
    weights = probs.astype(jnp.bfloat16)
    output = dot_nn(weights, value).astype(jnp.bfloat16)
    delta = jnp.sum(
        grad.astype(jnp.float32) * output.astype(jnp.float32), axis=1, keepdims=True
    )
    dscores = (probs * (dot_nt(grad, value) - delta)).astype(jnp.bfloat16)
    dquery = (dot_nn(dscores, key) * factor).astype(jnp.bfloat16)
    return output, dquery, dscores, weights


def route_kernel(
    labels_ref, qkv_hbm, grad_hbm, buffer_hbm, target_hbm, qkv_ref, grad_ref, buffer_ref, target_ref, sems
):
    tokens = labels_ref.shape[1]
    clusters = buffer_ref.shape[0]
    loads = [
        pltpu.make_async_copy(qkv_hbm, qkv_ref, sems.at[0]),
        pltpu.make_async_copy(grad_hbm, grad_ref, sems.at[1]),
    ]
    for load in loads:
        load.start()
    labels = labels_ref[...]
    block = 256
    lower = lax.broadcasted_iota(jnp.int32, (block, block), 0)
    upper = lax.broadcasted_iota(jnp.int32, (block, block), 1)
    triangle = (lower <= upper).astype(jnp.bfloat16)
    cluster_rows = lax.broadcasted_iota(jnp.int32, (clusters, block), 0)
    running = jnp.zeros((clusters, 1), jnp.float32)
    targets = []
    for start in range(0, tokens, block):
        part = labels[:, start : start + block]
        onehot = (cluster_rows == part).astype(jnp.float32)
        within = dot_nn(onehot.astype(jnp.bfloat16), triangle) + running
        rank = jnp.sum(within * onehot, axis=0, keepdims=True).astype(jnp.int32) - 1
        targets.append(part * SLOTS + rank)
        running = running + jnp.sum(onehot, axis=1, keepdims=True)
    target = jnp.concatenate(targets, axis=1)
    target_ref[...] = jnp.transpose(
        jnp.broadcast_to(target.astype(jnp.float32), (128, tokens))
    ).astype(jnp.int32)
    stores = [pltpu.make_async_copy(target_ref, target_hbm, sems.at[2])]
    stores[0].start()
    for load in loads:
        load.wait()
    payload = jnp.concatenate([qkv_ref[0], qkv_ref[1], qkv_ref[2], grad_ref[...]], axis=1)
    head_size = grad_ref.shape[1]
    slot_rows = lax.broadcasted_iota(jnp.int32, (SLOTS, tokens), 0)
    fill_rows = lax.broadcasted_iota(jnp.int32, (SLOTS, head_size), 0)
    for cluster in range(clusters):
        select = (slot_rows + cluster * SLOTS == target).astype(jnp.float32).astype(jnp.bfloat16)
        rows = dot_nn(select, payload)
        count = running[cluster : cluster + 1, :].astype(jnp.int32)
        first = jnp.where(fill_rows < count, rows[:, :head_size], EMPTY)
        buffer_ref[cluster, :, :head_size] = first.astype(jnp.bfloat16)
        buffer_ref[cluster, :, head_size:] = rows[:, head_size:].astype(jnp.bfloat16)
        store = pltpu.make_async_copy(
            buffer_ref.at[cluster], buffer_hbm.at[cluster], sems.at[3 + cluster]
        )
        store.start()
        stores.append(store)
    for store in stores:
        store.wait()


def route(labels, qkv, grad, clusters):
    tokens, head_size = grad.shape
    kept = pl.BlockSpec(memory_space=pl.ANY)
    return pl.pallas_call(
        route_kernel,
        out_shape=(
            jax.ShapeDtypeStruct((clusters, SLOTS, 4 * head_size), jnp.bfloat16),
            jax.ShapeDtypeStruct((tokens, 128), jnp.int32),
        ),
        in_specs=[pl.BlockSpec(memory_space=pltpu.VMEM), kept, kept],
        out_specs=(kept, kept),
        scratch_shapes=[
            pltpu.VMEM(qkv.shape, qkv.dtype),
            pltpu.VMEM(grad.shape, grad.dtype),
            pltpu.VMEM((clusters, SLOTS, 4 * head_size), jnp.bfloat16),
            pltpu.VMEM((tokens, 128), jnp.int32),
            pltpu.SemaphoreType.DMA((3 + clusters,)),
        ],
        compiler_params=pltpu.CompilerParams(vmem_limit_bytes=20 << 20),
        name="route",
    )(labels, qkv, grad)


def cluster_kernel(
    received_ref, result_hbm, counts_vmem, counts_smem, rows_ref, out_ref, result_ref, sem, sems
):
    sources = received_ref.shape[0]
    head_size = received_ref.shape[2] // 4
    tokens = rows_ref.shape[1] - SLOTS
    factor = head_size ** (-0.5)
    filled = []
    for source in range(sources):
        mark = received_ref[source, :, :head_size].astype(jnp.float32)
        filled.append(jnp.sum((mark < EMPTY).astype(jnp.float32), axis=0, keepdims=True))
    counts_vmem[...] = jnp.concatenate(filled, axis=0).astype(jnp.int32)
    copy = pltpu.make_async_copy(counts_vmem, counts_smem, sem)
    copy.start()
    copy.wait()
    starts = []
    start = 0
    for source in range(sources):
        starts.append(start)
        for part in range(4):
            lanes = slice(part * head_size, (part + 1) * head_size)
            rows_ref[part, pl.ds(start, SLOTS), :] = received_ref[source, :, lanes].astype(
                jnp.float32
            )
        start = jnp.minimum(start + counts_smem[source, 0], tokens)
    block = 256
    key = rows_ref[1, :tokens, :].astype(jnp.bfloat16)
    value = rows_ref[2, :tokens, :].astype(jnp.bfloat16)
    key_grad = jnp.zeros((tokens, head_size), jnp.float32)
    value_grad = jnp.zeros((tokens, head_size), jnp.float32)
    for row in range(0, tokens, block):
        query = rows_ref[0, row : row + block, :].astype(jnp.bfloat16)
        grad = rows_ref[3, row : row + block, :].astype(jnp.bfloat16)
        output, dquery, dscores, weights = softmax_grad(query, key, value, grad, factor, None)
        out_ref[0, row : row + block, :] = output.astype(jnp.float32)
        out_ref[1, row : row + block, :] = dquery.astype(jnp.float32)
        key_grad = key_grad + dot_tn(dscores, query)
        value_grad = value_grad + dot_tn(weights, grad)
    out_ref[2, :tokens, :] = key_grad * factor
    out_ref[3, :tokens, :] = value_grad
    out_ref[:, tokens:, :] = jnp.zeros((4, SLOTS, head_size), jnp.float32)
    stores = []
    for source in range(sources):
        for part in range(4):
            lanes = slice(part * head_size, (part + 1) * head_size)
            result_ref[source, :, lanes] = out_ref[part, pl.ds(starts[source], SLOTS), :].astype(
                jnp.bfloat16
            )
        store = pltpu.make_async_copy(
            result_ref.at[source], result_hbm.at[source], sems.at[source]
        )
        store.start()
        stores.append(store)
    for store in stores:
        store.wait()


def cluster_attention(received, tokens):
    sources, slots, width = received.shape
    vmem = pl.BlockSpec(memory_space=pltpu.VMEM)
    return pl.pallas_call(
        cluster_kernel,
        out_shape=jax.ShapeDtypeStruct(received.shape, jnp.bfloat16),
        in_specs=[vmem],
        out_specs=pl.BlockSpec(memory_space=pl.ANY),
        scratch_shapes=[
            pltpu.VMEM((sources, 128), jnp.int32),
            pltpu.SMEM((sources, 128), jnp.int32),
            pltpu.VMEM((4, tokens + SLOTS, width // 4), jnp.float32),
            pltpu.VMEM((4, tokens + SLOTS, width // 4), jnp.float32),
            pltpu.VMEM(received.shape, jnp.bfloat16),
            pltpu.SemaphoreType.DMA,
            pltpu.SemaphoreType.DMA((sources,)),
        ],
        compiler_params=pltpu.CompilerParams(vmem_limit_bytes=28 << 20),
        name="cluster",
    )(received)


def unroute_kernel(
    returned_ref, target_ref, output_hbm, grads_hbm, output_ref, grads_ref, sems
):
    clusters = returned_ref.shape[0]
    tokens, head_size = output_ref.shape
    slots = clusters * SLOTS
    rows = returned_ref[...].reshape(slots, 4 * head_size)
    block = 256
    lanes = lax.broadcasted_iota(jnp.int32, (block, 128), 1)
    stores = []
    for row in range(0, tokens, block):
        target = target_ref[row : row + block, :]
        select = jnp.concatenate(
            [
                (lanes + lane == target).astype(jnp.float32).astype(jnp.bfloat16)
                for lane in range(0, slots, 128)
            ],
            axis=1,
        )
        picked = dot_nn(select, rows).astype(jnp.bfloat16)
        output_ref[row : row + block, :] = picked[:, :head_size]
        for part in range(3):
            grads_ref[part, row : row + block, :] = picked[
                :, (part + 1) * head_size : (part + 2) * head_size
            ]
        span = pl.ds(row, block)
        step = row // block
        for store in (
            pltpu.make_async_copy(output_ref.at[span], output_hbm.at[span], sems.at[0, step]),
            pltpu.make_async_copy(grads_ref.at[:, span], grads_hbm.at[:, span], sems.at[1, step]),
        ):
            store.start()
            stores.append(store)
    for store in stores:
        store.wait()


def unroute(returned, target, head_size):
    tokens = target.shape[0]
    return pl.pallas_call(
        unroute_kernel,
        out_shape=(
            jax.ShapeDtypeStruct((tokens, head_size), jnp.bfloat16),
            jax.ShapeDtypeStruct((3, tokens, head_size), jnp.bfloat16),
        ),
        in_specs=[pl.BlockSpec(memory_space=pltpu.VMEM)] * 2,
        out_specs=(pl.BlockSpec(memory_space=pl.ANY),) * 2,
        scratch_shapes=[
            pltpu.VMEM((tokens, head_size), jnp.bfloat16),
            pltpu.VMEM((3, tokens, head_size), jnp.bfloat16),
            pltpu.SemaphoreType.DMA((2, 4)),
        ],
        compiler_params=pltpu.CompilerParams(vmem_limit_bytes=20 << 20),
        name="unroute",
    )(returned, target)


def local_kernel(
    index_ref, qkv_ref, grad_ref, prev_ref, output_ref, dquery_ref, own_ref, late_ref, keys, values, key_acc, value_acc
):
    tokens, head_size = grad_ref.shape
    factor = head_size ** (-0.5)
    block = 256
    span = WIN + block
    keys[:tokens, :] = prev_ref[0]
    keys[tokens:, :] = qkv_ref[1]
    values[:tokens, :] = prev_ref[1]
    values[tokens:, :] = qkv_ref[2]
    key_acc[...] = jnp.zeros_like(key_acc)
    value_acc[...] = jnp.zeros_like(value_acc)
    rows = lax.broadcasted_iota(jnp.int32, (block, block), 0)
    columns = lax.broadcasted_iota(jnp.int32, (block, block), 1)
    whole = lax.broadcasted_iota(jnp.int32, (block, span), 1)
    first_key = jnp.where(index_ref[0] == 0, tokens, 0)

    for row in range(0, tokens, block):

        def mask(scores, row=row):
            head = jnp.where(columns > rows, scores[:, :block], masked_fill)
            tail = jnp.where(columns <= rows, scores[:, span - block :], masked_fill)
            joined = jnp.concatenate([head, scores[:, block : span - block], tail], axis=1)
            return jnp.where(whole + row >= first_key, joined, masked_fill)

        query = qkv_ref[0, row : row + block, :]
        grad = grad_ref[row : row + block, :]
        key = keys[row : row + span, :]
        value = values[row : row + span, :]
        output, dquery, dscores, weights = softmax_grad(query, key, value, grad, factor, mask)
        output_ref[row : row + block, :] = output
        dquery_ref[row : row + block, :] = dquery
        key_acc[row : row + span, :] += dot_tn(dscores, query)
        value_acc[row : row + span, :] += dot_tn(weights, grad)
    late_ref[0] = (key_acc[:tokens, :] * factor).astype(jnp.bfloat16)
    late_ref[1] = value_acc[:tokens, :].astype(jnp.bfloat16)
    own_ref[0] = key_acc[tokens:, :] * factor
    own_ref[1] = value_acc[tokens:, :]


def local_attention(index, qkv, grad, prev):
    tokens, head_size = grad.shape
    vmem = pl.BlockSpec(memory_space=pltpu.VMEM)
    return pl.pallas_call(
        local_kernel,
        out_shape=(
            jax.ShapeDtypeStruct((tokens, head_size), jnp.bfloat16),
            jax.ShapeDtypeStruct((tokens, head_size), jnp.bfloat16),
            jax.ShapeDtypeStruct((2, tokens, head_size), jnp.float32),
            jax.ShapeDtypeStruct((2, tokens, head_size), jnp.bfloat16),
        ),
        in_specs=[pl.BlockSpec(memory_space=pltpu.SMEM), vmem, vmem, vmem],
        scratch_shapes=[
            pltpu.VMEM((2 * tokens, head_size), jnp.bfloat16),
            pltpu.VMEM((2 * tokens, head_size), jnp.bfloat16),
            pltpu.VMEM((2 * tokens, head_size), jnp.float32),
            pltpu.VMEM((2 * tokens, head_size), jnp.float32),
        ],
        compiler_params=pltpu.CompilerParams(vmem_limit_bytes=28 << 20),
        name="local",
    )(index, qkv, grad, prev)


def shifted(block, distance):
    devices = range(lax.axis_size("seq"))
    return lax.ppermute(
        block, "seq", [(i - distance, i) for i in devices if i - distance in devices]
    )


def exchange(block):
    return lax.all_to_all(block, "seq", split_axis=0, concat_axis=0, tiled=True)


def routed_first(local_qkv, local_grad, routed_qkv, routed_grad, cluster_ids):
    tokens, head_size = local_grad.shape
    buffer, target = route(cluster_ids, routed_qkv, routed_grad, lax.axis_size("seq"))
    received = exchange(buffer)
    halo, buffer = lax.optimization_barrier((local_qkv[1:], buffer))
    prev = shifted(halo, 1)
    result = cluster_attention(received, tokens)
    result, prev = lax.optimization_barrier((result, prev))
    returned = exchange(result)
    index = lax.axis_index("seq").astype(jnp.int32).reshape(1)
    local_out, dquery, own, late = local_attention(index, local_qkv, local_grad, prev)
    late = shifted(late, -1)
    joined = (own + late.astype(jnp.float32)).astype(jnp.bfloat16)
    local_dqkv = jnp.concatenate([dquery[None], joined], axis=0)
    routed_out, routed_dqkv = unroute(returned, target, head_size)
    return (local_out, local_dqkv, routed_out, routed_dqkv)


def local_first(local_qkv, local_grad, routed_qkv, routed_grad, cluster_ids):
    tokens, head_size = local_grad.shape
    buffer, target = route(cluster_ids, routed_qkv, routed_grad, lax.axis_size("seq"))
    halo, buffer = lax.optimization_barrier((local_qkv[1:], buffer))
    prev = shifted(halo, 1)
    index = lax.axis_index("seq").astype(jnp.int32).reshape(1)
    local_out, dquery, own, late = local_attention(index, local_qkv, local_grad, prev)
    buffer, late = lax.optimization_barrier((buffer, late))
    received = exchange(buffer)
    late = shifted(late, -1)
    result = cluster_attention(received, tokens)
    result, late = lax.optimization_barrier((result, late))
    returned = exchange(result)
    joined = (own + late.astype(jnp.float32)).astype(jnp.bfloat16)
    local_dqkv = jnp.concatenate([dquery[None], joined], axis=0)
    routed_out, routed_dqkv = unroute(returned, target, head_size)
    return (local_out, local_dqkv, routed_out, routed_dqkv)


def on_device(*arrays):
    return lax.cond(lax.axis_index("dp") == 0, routed_first, local_first, *arrays)


def solution(mesh):
    rows = P(("dp", "seq"), "head")
    stacked = P(None, ("dp", "seq"), "head")
    return jax.shard_map(
        on_device,
        mesh=mesh,
        in_specs=(stacked, rows, stacked, rows, P("head", ("dp", "seq"))),
        out_specs=(rows, stacked, rows, stacked),
        check_vma=False,
    )
```

```python
import jax
import jax.numpy as jnp
from jax import lax
from jax.experimental import pallas as pl
from jax.experimental.pallas import tpu as pltpu
from jax.sharding import PartitionSpec as P

WIN = 1024
SLOTS = 96
EMPTY = 512.0
masked_fill = -1e30
LOCAL_FLOPS = 10 * 1024 * 1280 * 128
HIDDEN_FLOPS = 200 * 10**9


def dot_nn(a, b):
    return lax.dot_general(a, b, (((1,), (0,)), ((), ())), preferred_element_type=jnp.float32)


def dot_nt(a, b):
    return lax.dot_general(a, b, (((1,), (1,)), ((), ())), preferred_element_type=jnp.float32)


def dot_tn(a, b):
    return lax.dot_general(a, b, (((0,), (0,)), ((), ())), preferred_element_type=jnp.float32)


def softmax_grad(query, key, value, grad, factor, mask):
    scores = dot_nt(query, key)
    if mask is not None:
        scores = mask(scores)
    peak = jnp.max(scores, axis=1, keepdims=True)
    probs = jnp.exp((scores - peak) * factor)
    probs = probs * (1.0 / jnp.sum(probs, axis=1, keepdims=True))
    weights = probs.astype(jnp.bfloat16)
    output = dot_nn(weights, value).astype(jnp.bfloat16)
    delta = jnp.sum(
        grad.astype(jnp.float32) * output.astype(jnp.float32), axis=1, keepdims=True
    )
    dscores = (probs * (dot_nt(grad, value) - delta)).astype(jnp.bfloat16)
    dquery = (dot_nn(dscores, key) * factor).astype(jnp.bfloat16)
    return output, dquery, dscores, weights


def route_kernel(
    labels_ref, qkv_hbm, grad_hbm, buffer_hbm, target_hbm, qkv_ref, grad_ref, buffer_ref, target_ref, sems
):
    tokens = labels_ref.shape[1]
    clusters = buffer_ref.shape[0]
    loads = [
        pltpu.make_async_copy(qkv_hbm, qkv_ref, sems.at[0]),
        pltpu.make_async_copy(grad_hbm, grad_ref, sems.at[1]),
    ]
    for load in loads:
        load.start()
    labels = labels_ref[...]
    block = 256
    lower = lax.broadcasted_iota(jnp.int32, (block, block), 0)
    upper = lax.broadcasted_iota(jnp.int32, (block, block), 1)
    triangle = (lower <= upper).astype(jnp.bfloat16)
    cluster_rows = lax.broadcasted_iota(jnp.int32, (clusters, block), 0)
    running = jnp.zeros((clusters, 1), jnp.float32)
    targets = []
    for start in range(0, tokens, block):
        part = labels[:, start : start + block]
        onehot = (cluster_rows == part).astype(jnp.float32)
        within = dot_nn(onehot.astype(jnp.bfloat16), triangle) + running
        rank = jnp.sum(within * onehot, axis=0, keepdims=True).astype(jnp.int32) - 1
        targets.append(part * SLOTS + rank)
        running = running + jnp.sum(onehot, axis=1, keepdims=True)
    target = jnp.concatenate(targets, axis=1)
    target_ref[...] = jnp.transpose(
        jnp.broadcast_to(target.astype(jnp.float32), (128, tokens))
    ).astype(jnp.int32)
    stores = [pltpu.make_async_copy(target_ref, target_hbm, sems.at[2])]
    stores[0].start()
    for load in loads:
        load.wait()
    payload = jnp.concatenate([qkv_ref[0], qkv_ref[1], qkv_ref[2], grad_ref[...]], axis=1)
    head_size = grad_ref.shape[1]
    slot_rows = lax.broadcasted_iota(jnp.int32, (SLOTS, tokens), 0)
    fill_rows = lax.broadcasted_iota(jnp.int32, (SLOTS, head_size), 0)
    for cluster in range(clusters):
        select = (slot_rows + cluster * SLOTS == target).astype(jnp.float32).astype(jnp.bfloat16)
        rows = dot_nn(select, payload)
        count = running[cluster : cluster + 1, :].astype(jnp.int32)
        first = jnp.where(fill_rows < count, rows[:, :head_size], EMPTY)
        buffer_ref[cluster, :, :head_size] = first.astype(jnp.bfloat16)
        buffer_ref[cluster, :, head_size:] = rows[:, head_size:].astype(jnp.bfloat16)
        store = pltpu.make_async_copy(
            buffer_ref.at[cluster], buffer_hbm.at[cluster], sems.at[3 + cluster]
        )
        store.start()
        stores.append(store)
    for store in stores:
        store.wait()


def route(labels, qkv, grad, clusters):
    tokens, head_size = grad.shape
    kept = pl.BlockSpec(memory_space=pl.ANY)
    return pl.pallas_call(
        route_kernel,
        out_shape=(
            jax.ShapeDtypeStruct((clusters, SLOTS, 4 * head_size), jnp.bfloat16),
            jax.ShapeDtypeStruct((tokens, 128), jnp.int32),
        ),
        in_specs=[pl.BlockSpec(memory_space=pltpu.VMEM), kept, kept],
        out_specs=(kept, kept),
        scratch_shapes=[
            pltpu.VMEM(qkv.shape, qkv.dtype),
            pltpu.VMEM(grad.shape, grad.dtype),
            pltpu.VMEM((clusters, SLOTS, 4 * head_size), jnp.bfloat16),
            pltpu.VMEM((tokens, 128), jnp.int32),
            pltpu.SemaphoreType.DMA((3 + clusters,)),
        ],
        compiler_params=pltpu.CompilerParams(vmem_limit_bytes=20 << 20),
        name="route",
    )(labels, qkv, grad)


def cluster_kernel(
    received_ref, result_hbm, counts_vmem, counts_smem, rows_ref, out_ref, result_ref, sem, sems
):
    sources = received_ref.shape[0]
    head_size = received_ref.shape[2] // 4
    tokens = rows_ref.shape[1] - SLOTS
    factor = head_size ** (-0.5)
    filled = []
    for source in range(sources):
        mark = received_ref[source, :, :head_size].astype(jnp.float32)
        filled.append(jnp.sum((mark < EMPTY).astype(jnp.float32), axis=0, keepdims=True))
    counts_vmem[...] = jnp.concatenate(filled, axis=0).astype(jnp.int32)
    copy = pltpu.make_async_copy(counts_vmem, counts_smem, sem)
    copy.start()
    copy.wait()
    starts = []
    start = 0
    for source in range(sources):
        starts.append(start)
        for part in range(4):
            lanes = slice(part * head_size, (part + 1) * head_size)
            rows_ref[part, pl.ds(start, SLOTS), :] = received_ref[source, :, lanes].astype(
                jnp.float32
            )
        start = jnp.minimum(start + counts_smem[source, 0], tokens)
    block = 256
    key = rows_ref[1, :tokens, :].astype(jnp.bfloat16)
    value = rows_ref[2, :tokens, :].astype(jnp.bfloat16)
    key_grad = jnp.zeros((tokens, head_size), jnp.float32)
    value_grad = jnp.zeros((tokens, head_size), jnp.float32)
    for row in range(0, tokens, block):
        query = rows_ref[0, row : row + block, :].astype(jnp.bfloat16)
        grad = rows_ref[3, row : row + block, :].astype(jnp.bfloat16)
        output, dquery, dscores, weights = softmax_grad(query, key, value, grad, factor, None)
        out_ref[0, row : row + block, :] = output.astype(jnp.float32)
        out_ref[1, row : row + block, :] = dquery.astype(jnp.float32)
        key_grad = key_grad + dot_tn(dscores, query)
        value_grad = value_grad + dot_tn(weights, grad)
    out_ref[2, :tokens, :] = key_grad * factor
    out_ref[3, :tokens, :] = value_grad
    out_ref[:, tokens:, :] = jnp.zeros((4, SLOTS, head_size), jnp.float32)
    stores = []
    for source in range(sources):
        for part in range(4):
            lanes = slice(part * head_size, (part + 1) * head_size)
            result_ref[source, :, lanes] = out_ref[part, pl.ds(starts[source], SLOTS), :].astype(
                jnp.bfloat16
            )
        store = pltpu.make_async_copy(
            result_ref.at[source], result_hbm.at[source], sems.at[source]
        )
        store.start()
        stores.append(store)
    for store in stores:
        store.wait()


def cluster_attention(received, tokens):
    sources, slots, width = received.shape
    vmem = pl.BlockSpec(memory_space=pltpu.VMEM)
    return pl.pallas_call(
        cluster_kernel,
        out_shape=jax.ShapeDtypeStruct(received.shape, jnp.bfloat16),
        in_specs=[vmem],
        out_specs=pl.BlockSpec(memory_space=pl.ANY),
        scratch_shapes=[
            pltpu.VMEM((sources, 128), jnp.int32),
            pltpu.SMEM((sources, 128), jnp.int32),
            pltpu.VMEM((4, tokens + SLOTS, width // 4), jnp.float32),
            pltpu.VMEM((4, tokens + SLOTS, width // 4), jnp.float32),
            pltpu.VMEM(received.shape, jnp.bfloat16),
            pltpu.SemaphoreType.DMA,
            pltpu.SemaphoreType.DMA((sources,)),
        ],
        compiler_params=pltpu.CompilerParams(vmem_limit_bytes=28 << 20),
        name="cluster",
    )(received)


def unroute_kernel(
    returned_ref, target_ref, output_hbm, grads_hbm, output_ref, grads_ref, sems
):
    clusters = returned_ref.shape[0]
    tokens, head_size = output_ref.shape
    slots = clusters * SLOTS
    rows = returned_ref[...].reshape(slots, 4 * head_size)
    block = 256
    lanes = lax.broadcasted_iota(jnp.int32, (block, 128), 1)
    stores = []
    for row in range(0, tokens, block):
        target = target_ref[row : row + block, :]
        select = jnp.concatenate(
            [
                (lanes + lane == target).astype(jnp.float32).astype(jnp.bfloat16)
                for lane in range(0, slots, 128)
            ],
            axis=1,
        )
        picked = dot_nn(select, rows).astype(jnp.bfloat16)
        output_ref[row : row + block, :] = picked[:, :head_size]
        for part in range(3):
            grads_ref[part, row : row + block, :] = picked[
                :, (part + 1) * head_size : (part + 2) * head_size
            ]
        span = pl.ds(row, block)
        step = row // block
        for store in (
            pltpu.make_async_copy(output_ref.at[span], output_hbm.at[span], sems.at[0, step]),
            pltpu.make_async_copy(grads_ref.at[:, span], grads_hbm.at[:, span], sems.at[1, step]),
        ):
            store.start()
            stores.append(store)
    for store in stores:
        store.wait()


def unroute(returned, target, head_size):
    tokens = target.shape[0]
    return pl.pallas_call(
        unroute_kernel,
        out_shape=(
            jax.ShapeDtypeStruct((tokens, head_size), jnp.bfloat16),
            jax.ShapeDtypeStruct((3, tokens, head_size), jnp.bfloat16),
        ),
        in_specs=[pl.BlockSpec(memory_space=pltpu.VMEM)] * 2,
        out_specs=(pl.BlockSpec(memory_space=pl.ANY),) * 2,
        scratch_shapes=[
            pltpu.VMEM((tokens, head_size), jnp.bfloat16),
            pltpu.VMEM((3, tokens, head_size), jnp.bfloat16),
            pltpu.SemaphoreType.DMA((2, 4)),
        ],
        compiler_params=pltpu.CompilerParams(vmem_limit_bytes=20 << 20),
        name="unroute",
    )(returned, target)


def local_kernel(
    index_ref, qkv_ref, grad_ref, prev_ref, output_ref, dquery_ref, own_ref, late_ref, keys, values, key_acc, value_acc
):
    tokens, head_size = grad_ref.shape
    factor = head_size ** (-0.5)
    block = 256
    span = WIN + block
    keys[:tokens, :] = prev_ref[0]
    keys[tokens:, :] = qkv_ref[1]
    values[:tokens, :] = prev_ref[1]
    values[tokens:, :] = qkv_ref[2]
    key_acc[...] = jnp.zeros_like(key_acc)
    value_acc[...] = jnp.zeros_like(value_acc)
    rows = lax.broadcasted_iota(jnp.int32, (block, block), 0)
    columns = lax.broadcasted_iota(jnp.int32, (block, block), 1)
    whole = lax.broadcasted_iota(jnp.int32, (block, span), 1)
    first_key = jnp.where(index_ref[0] == 0, tokens, 0)

    for row in range(0, tokens, block):

        def mask(scores, row=row):
            head = jnp.where(columns > rows, scores[:, :block], masked_fill)
            tail = jnp.where(columns <= rows, scores[:, span - block :], masked_fill)
            joined = jnp.concatenate([head, scores[:, block : span - block], tail], axis=1)
            return jnp.where(whole + row >= first_key, joined, masked_fill)

        query = qkv_ref[0, row : row + block, :]
        grad = grad_ref[row : row + block, :]
        key = keys[row : row + span, :]
        value = values[row : row + span, :]
        output, dquery, dscores, weights = softmax_grad(query, key, value, grad, factor, mask)
        output_ref[row : row + block, :] = output
        dquery_ref[row : row + block, :] = dquery
        key_acc[row : row + span, :] += dot_tn(dscores, query)
        value_acc[row : row + span, :] += dot_tn(weights, grad)
    late_ref[0] = (key_acc[:tokens, :] * factor).astype(jnp.bfloat16)
    late_ref[1] = value_acc[:tokens, :].astype(jnp.bfloat16)
    own_ref[0] = key_acc[tokens:, :] * factor
    own_ref[1] = value_acc[tokens:, :]


def local_attention(index, qkv, grad, prev, cost):
    tokens, head_size = grad.shape
    vmem = pl.BlockSpec(memory_space=pltpu.VMEM)
    return pl.pallas_call(
        local_kernel,
        out_shape=(
            jax.ShapeDtypeStruct((tokens, head_size), jnp.bfloat16),
            jax.ShapeDtypeStruct((tokens, head_size), jnp.bfloat16),
            jax.ShapeDtypeStruct((2, tokens, head_size), jnp.float32),
            jax.ShapeDtypeStruct((2, tokens, head_size), jnp.bfloat16),
        ),
        in_specs=[pl.BlockSpec(memory_space=pltpu.SMEM), vmem, vmem, vmem],
        scratch_shapes=[
            pltpu.VMEM((2 * tokens, head_size), jnp.bfloat16),
            pltpu.VMEM((2 * tokens, head_size), jnp.bfloat16),
            pltpu.VMEM((2 * tokens, head_size), jnp.float32),
            pltpu.VMEM((2 * tokens, head_size), jnp.float32),
        ],
        compiler_params=pltpu.CompilerParams(vmem_limit_bytes=28 << 20),
        cost_estimate=pl.CostEstimate(
            flops=cost, transcendentals=tokens * (WIN + 256), bytes_accessed=12 * tokens * head_size
        ),
        name="local",
    )(index, qkv, grad, prev)


def shifted(block, distance):
    devices = range(lax.axis_size("seq"))
    return lax.ppermute(
        block, "seq", [(i - distance, i) for i in devices if i - distance in devices]
    )


def exchange(block):
    return lax.all_to_all(block, "seq", split_axis=0, concat_axis=0, tiled=True)


def routed_first(local_qkv, local_grad, routed_qkv, routed_grad, cluster_ids):
    tokens, head_size = local_grad.shape
    buffer, target = route(cluster_ids, routed_qkv, routed_grad, lax.axis_size("seq"))
    received = exchange(buffer)
    halo, buffer = lax.optimization_barrier((local_qkv[1:], buffer))
    prev = shifted(halo, 1)
    result = cluster_attention(received, tokens)
    returned = exchange(result)
    index = lax.axis_index("seq").astype(jnp.int32).reshape(1)
    local_out, dquery, own, late = local_attention(
        index, local_qkv, local_grad, prev, HIDDEN_FLOPS
    )
    late = shifted(late, -1)
    joined = (own + late.astype(jnp.float32)).astype(jnp.bfloat16)
    local_dqkv = jnp.concatenate([dquery[None], joined], axis=0)
    routed_out, routed_dqkv = unroute(returned, target, head_size)
    return (local_out, local_dqkv, routed_out, routed_dqkv)


def local_first(local_qkv, local_grad, routed_qkv, routed_grad, cluster_ids):
    tokens, head_size = local_grad.shape
    buffer, target = route(cluster_ids, routed_qkv, routed_grad, lax.axis_size("seq"))
    halo, buffer = lax.optimization_barrier((local_qkv[1:], buffer))
    prev = shifted(halo, 1)
    index = lax.axis_index("seq").astype(jnp.int32).reshape(1)
    local_out, dquery, own, late = local_attention(
        index, local_qkv, local_grad, prev, LOCAL_FLOPS
    )
    buffer, late = lax.optimization_barrier((buffer, late))
    received = exchange(buffer)
    late = shifted(late, -1)
    result = cluster_attention(received, tokens)
    result, late = lax.optimization_barrier((result, late))
    returned = exchange(result)
    joined = (own + late.astype(jnp.float32)).astype(jnp.bfloat16)
    local_dqkv = jnp.concatenate([dquery[None], joined], axis=0)
    routed_out, routed_dqkv = unroute(returned, target, head_size)
    return (local_out, local_dqkv, routed_out, routed_dqkv)


def on_device(*arrays):
    return lax.cond(lax.axis_index("dp") == 0, routed_first, local_first, *arrays)


def solution(mesh):
    rows = P(("dp", "seq"), "head")
    stacked = P(None, ("dp", "seq"), "head")
    return jax.shard_map(
        on_device,
        mesh=mesh,
        in_specs=(stacked, rows, stacked, rows, P("head", ("dp", "seq"))),
        out_specs=(rows, stacked, rows, stacked),
        check_vma=False,
    )
```

```python
import jax
import jax.numpy as jnp
from jax import lax
from jax.experimental import pallas as pl
from jax.experimental.pallas import tpu as pltpu
from jax.sharding import PartitionSpec as P

WIN = 1024
SLOTS = 96
EMPTY = 512.0
masked_fill = -1e30
LOCAL_FLOPS = 10 * 1024 * 1280 * 128
HIDDEN_FLOPS = 200 * 10**9


def dot_nn(a, b):
    return lax.dot_general(a, b, (((1,), (0,)), ((), ())), preferred_element_type=jnp.float32)


def dot_nt(a, b):
    return lax.dot_general(a, b, (((1,), (1,)), ((), ())), preferred_element_type=jnp.float32)


def dot_tn(a, b):
    return lax.dot_general(a, b, (((0,), (0,)), ((), ())), preferred_element_type=jnp.float32)


def softmax_grad(query, key, value, grad, factor, mask):
    scores = dot_nt(query, key)
    if mask is not None:
        scores = mask(scores)
    peak = jnp.max(scores, axis=1, keepdims=True)
    probs = jnp.exp((scores - peak) * factor)
    probs = probs * (1.0 / jnp.sum(probs, axis=1, keepdims=True))
    weights = probs.astype(jnp.bfloat16)
    output = dot_nn(weights, value).astype(jnp.bfloat16)
    delta = jnp.sum(
        grad.astype(jnp.float32) * output.astype(jnp.float32), axis=1, keepdims=True
    )
    dscores = (probs * (dot_nt(grad, value) - delta)).astype(jnp.bfloat16)
    dquery = (dot_nn(dscores, key) * factor).astype(jnp.bfloat16)
    return output, dquery, dscores, weights


def route_kernel(
    labels_hbm,
    qkv_hbm,
    grad_hbm,
    buffer_hbm,
    target_hbm,
    labels_ref,
    qkv_ref,
    grad_ref,
    buffer_ref,
    target_ref,
    sems,
):
    tokens = labels_ref.shape[1]
    clusters = buffer_ref.shape[0]
    half = tokens // 2
    first_load = pltpu.make_async_copy(labels_hbm, labels_ref, sems.at[0])
    first_load.start()
    loads = []
    for part in range(4):
        for piece in range(2):
            rows = pl.ds(piece * half, half)
            if part < 3:
                pair = (qkv_hbm.at[part, rows], qkv_ref.at[part, rows])
            else:
                pair = (grad_hbm.at[rows], grad_ref.at[rows])
            loads.append(pltpu.make_async_copy(*pair, sems.at[2 + 2 * part + piece]))
    for load in loads:
        load.start()
    block = 256
    lower = lax.broadcasted_iota(jnp.int32, (block, block), 0)
    upper = lax.broadcasted_iota(jnp.int32, (block, block), 1)
    triangle = (lower <= upper).astype(jnp.bfloat16)
    cluster_rows = lax.broadcasted_iota(jnp.int32, (clusters, block), 0)
    running = jnp.zeros((clusters, 1), jnp.float32)
    targets = []
    first_load.wait()
    labels = labels_ref[...]
    for start in range(0, tokens, block):
        part = labels[:, start : start + block]
        onehot = (cluster_rows == part).astype(jnp.float32)
        within = dot_nn(onehot.astype(jnp.bfloat16), triangle) + running
        rank = jnp.sum(within * onehot, axis=0, keepdims=True).astype(jnp.int32) - 1
        targets.append(part * SLOTS + rank)
        running = running + jnp.sum(onehot, axis=1, keepdims=True)
    target = jnp.concatenate(targets, axis=1)
    target_ref[...] = jnp.transpose(
        jnp.broadcast_to(target.astype(jnp.float32), (128, tokens))
    ).astype(jnp.int32)
    stores = [pltpu.make_async_copy(target_ref, target_hbm, sems.at[1])]
    stores[0].start()
    for load in loads:
        load.wait()
    payload = jnp.concatenate([qkv_ref[0], qkv_ref[1], qkv_ref[2], grad_ref[...]], axis=1)
    head_size = grad_ref.shape[1]
    slot_rows = lax.broadcasted_iota(jnp.int32, (SLOTS, tokens), 0)
    fill_rows = lax.broadcasted_iota(jnp.int32, (SLOTS, head_size), 0)
    for cluster in range(clusters):
        select = (slot_rows + cluster * SLOTS == target).astype(jnp.float32).astype(jnp.bfloat16)
        rows = dot_nn(select, payload)
        count = running[cluster : cluster + 1, :].astype(jnp.int32)
        first = jnp.where(fill_rows < count, rows[:, :head_size], EMPTY)
        buffer_ref[cluster, :, :head_size] = first.astype(jnp.bfloat16)
        buffer_ref[cluster, :, head_size:] = rows[:, head_size:].astype(jnp.bfloat16)
        store = pltpu.make_async_copy(
            buffer_ref.at[cluster], buffer_hbm.at[cluster], sems.at[10 + cluster]
        )
        store.start()
        stores.append(store)
    for store in stores:
        store.wait()


def route(labels, qkv, grad, clusters):
    tokens, head_size = grad.shape
    kept = pl.BlockSpec(memory_space=pl.ANY)
    return pl.pallas_call(
        route_kernel,
        out_shape=(
            jax.ShapeDtypeStruct((clusters, SLOTS, 4 * head_size), jnp.bfloat16),
            jax.ShapeDtypeStruct((tokens, 128), jnp.int32),
        ),
        in_specs=[kept, kept, kept],
        out_specs=(kept, kept),
        scratch_shapes=[
            pltpu.VMEM(labels.shape, labels.dtype),
            pltpu.VMEM(qkv.shape, qkv.dtype),
            pltpu.VMEM(grad.shape, grad.dtype),
            pltpu.VMEM((clusters, SLOTS, 4 * head_size), jnp.bfloat16),
            pltpu.VMEM((tokens, 128), jnp.int32),
            pltpu.SemaphoreType.DMA((10 + clusters,)),
        ],
        compiler_params=pltpu.CompilerParams(vmem_limit_bytes=20 << 20),
        name="route",
    )(labels, qkv, grad)


def cluster_kernel(
    received_ref, result_hbm, counts_vmem, counts_smem, rows_ref, out_ref, result_ref, sem, sems
):
    sources = received_ref.shape[0]
    head_size = received_ref.shape[2] // 4
    tokens = rows_ref.shape[1] - SLOTS
    factor = head_size ** (-0.5)
    filled = []
    for source in range(sources):
        mark = received_ref[source, :, :head_size].astype(jnp.float32)
        filled.append(jnp.sum((mark < EMPTY).astype(jnp.float32), axis=0, keepdims=True))
    counts_vmem[...] = jnp.concatenate(filled, axis=0).astype(jnp.int32)
    copy = pltpu.make_async_copy(counts_vmem, counts_smem, sem)
    copy.start()
    copy.wait()
    starts = []
    start = 0
    for source in range(sources):
        starts.append(start)
        for part in range(4):
            lanes = slice(part * head_size, (part + 1) * head_size)
            rows_ref[part, pl.ds(start, SLOTS), :] = received_ref[source, :, lanes].astype(
                jnp.float32
            )
        start = jnp.minimum(start + counts_smem[source, 0], tokens)
    block = 256
    key = rows_ref[1, :tokens, :].astype(jnp.bfloat16)
    value = rows_ref[2, :tokens, :].astype(jnp.bfloat16)
    key_grad = jnp.zeros((tokens, head_size), jnp.float32)
    value_grad = jnp.zeros((tokens, head_size), jnp.float32)
    for row in range(0, tokens, block):
        query = rows_ref[0, row : row + block, :].astype(jnp.bfloat16)
        grad = rows_ref[3, row : row + block, :].astype(jnp.bfloat16)
        output, dquery, dscores, weights = softmax_grad(query, key, value, grad, factor, None)
        out_ref[0, row : row + block, :] = output.astype(jnp.float32)
        out_ref[1, row : row + block, :] = dquery.astype(jnp.float32)
        key_grad = key_grad + dot_tn(dscores, query)
        value_grad = value_grad + dot_tn(weights, grad)
    out_ref[2, :tokens, :] = key_grad * factor
    out_ref[3, :tokens, :] = value_grad
    out_ref[:, tokens:, :] = jnp.zeros((4, SLOTS, head_size), jnp.float32)
    stores = []
    for source in range(sources):
        for part in range(4):
            lanes = slice(part * head_size, (part + 1) * head_size)
            result_ref[source, :, lanes] = out_ref[part, pl.ds(starts[source], SLOTS), :].astype(
                jnp.bfloat16
            )
        store = pltpu.make_async_copy(
            result_ref.at[source], result_hbm.at[source], sems.at[source]
        )
        store.start()
        stores.append(store)
    for store in stores:
        store.wait()


def cluster_attention(received, tokens):
    sources, slots, width = received.shape
    vmem = pl.BlockSpec(memory_space=pltpu.VMEM)
    return pl.pallas_call(
        cluster_kernel,
        out_shape=jax.ShapeDtypeStruct(received.shape, jnp.bfloat16),
        in_specs=[vmem],
        out_specs=pl.BlockSpec(memory_space=pl.ANY),
        scratch_shapes=[
            pltpu.VMEM((sources, 128), jnp.int32),
            pltpu.SMEM((sources, 128), jnp.int32),
            pltpu.VMEM((4, tokens + SLOTS, width // 4), jnp.float32),
            pltpu.VMEM((4, tokens + SLOTS, width // 4), jnp.float32),
            pltpu.VMEM(received.shape, jnp.bfloat16),
            pltpu.SemaphoreType.DMA,
            pltpu.SemaphoreType.DMA((sources,)),
        ],
        compiler_params=pltpu.CompilerParams(vmem_limit_bytes=28 << 20),
        name="cluster",
    )(received)


def unroute_kernel(
    returned_ref, target_ref, output_hbm, grads_hbm, output_ref, grads_ref, sems
):
    clusters = returned_ref.shape[0]
    tokens, head_size = output_ref.shape
    slots = clusters * SLOTS
    rows = returned_ref[...].reshape(slots, 4 * head_size)
    block = 256
    lanes = lax.broadcasted_iota(jnp.int32, (block, 128), 1)
    stores = []
    for row in range(0, tokens, block):
        target = target_ref[row : row + block, :]
        select = jnp.concatenate(
            [
                (lanes + lane == target).astype(jnp.float32).astype(jnp.bfloat16)
                for lane in range(0, slots, 128)
            ],
            axis=1,
        )
        picked = dot_nn(select, rows).astype(jnp.bfloat16)
        output_ref[row : row + block, :] = picked[:, :head_size]
        for part in range(3):
            grads_ref[part, row : row + block, :] = picked[
                :, (part + 1) * head_size : (part + 2) * head_size
            ]
        span = pl.ds(row, block)
        step = row // block
        for store in (
            pltpu.make_async_copy(output_ref.at[span], output_hbm.at[span], sems.at[0, step]),
            pltpu.make_async_copy(grads_ref.at[:, span], grads_hbm.at[:, span], sems.at[1, step]),
        ):
            store.start()
            stores.append(store)
    for store in stores:
        store.wait()


def unroute(returned, target, head_size):
    tokens = target.shape[0]
    return pl.pallas_call(
        unroute_kernel,
        out_shape=(
            jax.ShapeDtypeStruct((tokens, head_size), jnp.bfloat16),
            jax.ShapeDtypeStruct((3, tokens, head_size), jnp.bfloat16),
        ),
        in_specs=[pl.BlockSpec(memory_space=pltpu.VMEM)] * 2,
        out_specs=(pl.BlockSpec(memory_space=pl.ANY),) * 2,
        scratch_shapes=[
            pltpu.VMEM((tokens, head_size), jnp.bfloat16),
            pltpu.VMEM((3, tokens, head_size), jnp.bfloat16),
            pltpu.SemaphoreType.DMA((2, 4)),
        ],
        compiler_params=pltpu.CompilerParams(vmem_limit_bytes=20 << 20),
        name="unroute",
    )(returned, target)


def local_kernel(
    index_ref, qkv_ref, grad_ref, prev_ref, output_ref, dquery_ref, own_ref, late_ref, keys, values, key_acc, value_acc
):
    tokens, head_size = grad_ref.shape
    factor = head_size ** (-0.5)
    block = 256
    span = WIN + block
    keys[:tokens, :] = prev_ref[0]
    keys[tokens:, :] = qkv_ref[1]
    values[:tokens, :] = prev_ref[1]
    values[tokens:, :] = qkv_ref[2]
    key_acc[...] = jnp.zeros_like(key_acc)
    value_acc[...] = jnp.zeros_like(value_acc)
    rows = lax.broadcasted_iota(jnp.int32, (block, block), 0)
    columns = lax.broadcasted_iota(jnp.int32, (block, block), 1)
    whole = lax.broadcasted_iota(jnp.int32, (block, span), 1)
    first_key = jnp.where(index_ref[0] == 0, tokens, 0)

    for row in range(0, tokens, block):

        def mask(scores, row=row):
            head = jnp.where(columns > rows, scores[:, :block], masked_fill)
            tail = jnp.where(columns <= rows, scores[:, span - block :], masked_fill)
            joined = jnp.concatenate([head, scores[:, block : span - block], tail], axis=1)
            return jnp.where(whole + row >= first_key, joined, masked_fill)

        query = qkv_ref[0, row : row + block, :]
        grad = grad_ref[row : row + block, :]
        key = keys[row : row + span, :]
        value = values[row : row + span, :]
        output, dquery, dscores, weights = softmax_grad(query, key, value, grad, factor, mask)
        output_ref[row : row + block, :] = output
        dquery_ref[row : row + block, :] = dquery
        key_acc[row : row + span, :] += dot_tn(dscores, query)
        value_acc[row : row + span, :] += dot_tn(weights, grad)
    late_ref[0] = (key_acc[:tokens, :] * factor).astype(jnp.bfloat16)
    late_ref[1] = value_acc[:tokens, :].astype(jnp.bfloat16)
    own_ref[0] = key_acc[tokens:, :] * factor
    own_ref[1] = value_acc[tokens:, :]


def local_attention(index, qkv, grad, prev, cost):
    tokens, head_size = grad.shape
    vmem = pl.BlockSpec(memory_space=pltpu.VMEM)
    return pl.pallas_call(
        local_kernel,
        out_shape=(
            jax.ShapeDtypeStruct((tokens, head_size), jnp.bfloat16),
            jax.ShapeDtypeStruct((tokens, head_size), jnp.bfloat16),
            jax.ShapeDtypeStruct((2, tokens, head_size), jnp.float32),
            jax.ShapeDtypeStruct((2, tokens, head_size), jnp.bfloat16),
        ),
        in_specs=[pl.BlockSpec(memory_space=pltpu.SMEM), vmem, vmem, vmem],
        scratch_shapes=[
            pltpu.VMEM((2 * tokens, head_size), jnp.bfloat16),
            pltpu.VMEM((2 * tokens, head_size), jnp.bfloat16),
            pltpu.VMEM((2 * tokens, head_size), jnp.float32),
            pltpu.VMEM((2 * tokens, head_size), jnp.float32),
        ],
        compiler_params=pltpu.CompilerParams(vmem_limit_bytes=28 << 20),
        cost_estimate=pl.CostEstimate(
            flops=cost, transcendentals=tokens * (WIN + 256), bytes_accessed=12 * tokens * head_size
        ),
        name="local",
    )(index, qkv, grad, prev)


def shifted(block, distance):
    devices = range(lax.axis_size("seq"))
    return lax.ppermute(
        block, "seq", [(i - distance, i) for i in devices if i - distance in devices]
    )


def exchange(block):
    return lax.all_to_all(block, "seq", split_axis=0, concat_axis=0, tiled=True)


def routed_first(local_qkv, local_grad, routed_qkv, routed_grad, cluster_ids):
    tokens, head_size = local_grad.shape
    buffer, target = route(cluster_ids, routed_qkv, routed_grad, lax.axis_size("seq"))
    received = exchange(buffer)
    halo, buffer = lax.optimization_barrier((local_qkv[1:], buffer))
    prev = shifted(halo, 1)
    result = cluster_attention(received, tokens)
    returned = exchange(result)
    index = lax.axis_index("seq").astype(jnp.int32).reshape(1)
    local_out, dquery, own, late = local_attention(
        index, local_qkv, local_grad, prev, HIDDEN_FLOPS
    )
    late = shifted(late, -1)
    joined = (own + late.astype(jnp.float32)).astype(jnp.bfloat16)
    local_dqkv = jnp.concatenate([dquery[None], joined], axis=0)
    routed_out, routed_dqkv = unroute(returned, target, head_size)
    return (local_out, local_dqkv, routed_out, routed_dqkv)


def local_first(local_qkv, local_grad, routed_qkv, routed_grad, cluster_ids):
    tokens, head_size = local_grad.shape
    buffer, target = route(cluster_ids, routed_qkv, routed_grad, lax.axis_size("seq"))
    halo, buffer = lax.optimization_barrier((local_qkv[1:], buffer))
    prev = shifted(halo, 1)
    index = lax.axis_index("seq").astype(jnp.int32).reshape(1)
    local_out, dquery, own, late = local_attention(
        index, local_qkv, local_grad, prev, LOCAL_FLOPS
    )
    buffer, late = lax.optimization_barrier((buffer, late))
    received = exchange(buffer)
    late = shifted(late, -1)
    result = cluster_attention(received, tokens)
    result, late = lax.optimization_barrier((result, late))
    returned = exchange(result)
    joined = (own + late.astype(jnp.float32)).astype(jnp.bfloat16)
    local_dqkv = jnp.concatenate([dquery[None], joined], axis=0)
    routed_out, routed_dqkv = unroute(returned, target, head_size)
    return (local_out, local_dqkv, routed_out, routed_dqkv)


def on_device(*arrays):
    return lax.cond(lax.axis_index("dp") == 0, routed_first, local_first, *arrays)


def solution(mesh):
    rows = P(("dp", "seq"), "head")
    stacked = P(None, ("dp", "seq"), "head")
    return jax.shard_map(
        on_device,
        mesh=mesh,
        in_specs=(stacked, rows, stacked, rows, P("head", ("dp", "seq"))),
        out_specs=(rows, stacked, rows, stacked),
        check_vma=False,
    )
```

```python
import jax
import jax.numpy as jnp
from jax import lax
from jax.experimental import pallas as pl
from jax.experimental.pallas import tpu as pltpu
from jax.sharding import PartitionSpec as P

WIN = 1024
SLOTS = 96
EMPTY = 512.0
masked_fill = -1e30
LOCAL_FLOPS = 10 * 1024 * 1280 * 128
HIDDEN_FLOPS = 100 * 10**9


def dot_nn(a, b):
    return lax.dot_general(a, b, (((1,), (0,)), ((), ())), preferred_element_type=jnp.float32)


def dot_nt(a, b):
    return lax.dot_general(a, b, (((1,), (1,)), ((), ())), preferred_element_type=jnp.float32)


def dot_tn(a, b):
    return lax.dot_general(a, b, (((0,), (0,)), ((), ())), preferred_element_type=jnp.float32)


def softmax_grad(query, key, value, grad, factor, mask):
    scores = dot_nt(query, key)
    if mask is not None:
        scores = mask(scores)
    peak = jnp.max(scores, axis=1, keepdims=True)
    probs = jnp.exp((scores - peak) * factor)
    probs = probs * (1.0 / jnp.sum(probs, axis=1, keepdims=True))
    weights = probs.astype(jnp.bfloat16)
    output = dot_nn(weights, value).astype(jnp.bfloat16)
    delta = jnp.sum(
        grad.astype(jnp.float32) * output.astype(jnp.float32), axis=1, keepdims=True
    )
    dscores = (probs * (dot_nt(grad, value) - delta)).astype(jnp.bfloat16)
    dquery = (dot_nn(dscores, key) * factor).astype(jnp.bfloat16)
    return output, dquery, dscores, weights


def route_kernel(
    labels_hbm,
    qkv_hbm,
    grad_hbm,
    buffer_hbm,
    target_hbm,
    labels_ref,
    qkv_ref,
    grad_ref,
    buffer_ref,
    target_ref,
    sems,
):
    tokens = labels_ref.shape[1]
    clusters = buffer_ref.shape[0]
    half = tokens // 2
    first_load = pltpu.make_async_copy(labels_hbm, labels_ref, sems.at[0])
    first_load.start()
    loads = []
    for part in range(4):
        for piece in range(2):
            rows = pl.ds(piece * half, half)
            if part < 3:
                pair = (qkv_hbm.at[part, rows], qkv_ref.at[part, rows])
            else:
                pair = (grad_hbm.at[rows], grad_ref.at[rows])
            loads.append(pltpu.make_async_copy(*pair, sems.at[2 + 2 * part + piece]))
    for load in loads:
        load.start()
    block = 256
    lower = lax.broadcasted_iota(jnp.int32, (block, block), 0)
    upper = lax.broadcasted_iota(jnp.int32, (block, block), 1)
    triangle = (lower <= upper).astype(jnp.bfloat16)
    cluster_rows = lax.broadcasted_iota(jnp.int32, (clusters, block), 0)
    running = jnp.zeros((clusters, 1), jnp.float32)
    targets = []
    first_load.wait()
    labels = labels_ref[...]
    for start in range(0, tokens, block):
        part = labels[:, start : start + block]
        onehot = (cluster_rows == part).astype(jnp.float32)
        within = dot_nn(onehot.astype(jnp.bfloat16), triangle) + running
        rank = jnp.sum(within * onehot, axis=0, keepdims=True).astype(jnp.int32) - 1
        targets.append(part * SLOTS + rank)
        running = running + jnp.sum(onehot, axis=1, keepdims=True)
    target = jnp.concatenate(targets, axis=1)
    target_ref[...] = jnp.transpose(
        jnp.broadcast_to(target.astype(jnp.float32), (128, tokens))
    ).astype(jnp.int32)
    stores = [pltpu.make_async_copy(target_ref, target_hbm, sems.at[1])]
    stores[0].start()
    for load in loads:
        load.wait()
    payload = jnp.concatenate([qkv_ref[0], qkv_ref[1], qkv_ref[2], grad_ref[...]], axis=1)
    head_size = grad_ref.shape[1]
    slot_rows = lax.broadcasted_iota(jnp.int32, (SLOTS, tokens), 0)
    fill_rows = lax.broadcasted_iota(jnp.int32, (SLOTS, head_size), 0)
    for cluster in range(clusters):
        select = (slot_rows + cluster * SLOTS == target).astype(jnp.float32).astype(jnp.bfloat16)
        rows = dot_nn(select, payload)
        count = running[cluster : cluster + 1, :].astype(jnp.int32)
        first = jnp.where(fill_rows < count, rows[:, :head_size], EMPTY)
        buffer_ref[cluster, :, :head_size] = first.astype(jnp.bfloat16)
        buffer_ref[cluster, :, head_size:] = rows[:, head_size:].astype(jnp.bfloat16)
        store = pltpu.make_async_copy(
            buffer_ref.at[cluster], buffer_hbm.at[cluster], sems.at[10 + cluster]
        )
        store.start()
        stores.append(store)
    for store in stores:
        store.wait()


def route(labels, qkv, grad, clusters):
    tokens, head_size = grad.shape
    kept = pl.BlockSpec(memory_space=pl.ANY)
    return pl.pallas_call(
        route_kernel,
        out_shape=(
            jax.ShapeDtypeStruct((clusters, SLOTS, 4 * head_size), jnp.bfloat16),
            jax.ShapeDtypeStruct((tokens, 128), jnp.int32),
        ),
        in_specs=[kept, kept, kept],
        out_specs=(kept, kept),
        scratch_shapes=[
            pltpu.VMEM(labels.shape, labels.dtype),
            pltpu.VMEM(qkv.shape, qkv.dtype),
            pltpu.VMEM(grad.shape, grad.dtype),
            pltpu.VMEM((clusters, SLOTS, 4 * head_size), jnp.bfloat16),
            pltpu.VMEM((tokens, 128), jnp.int32),
            pltpu.SemaphoreType.DMA((10 + clusters,)),
        ],
        compiler_params=pltpu.CompilerParams(vmem_limit_bytes=20 << 20),
        name="route",
    )(labels, qkv, grad)


def cluster_kernel(
    received_ref, result_hbm, counts_vmem, counts_smem, rows_ref, out_ref, result_ref, sem, sems
):
    sources = received_ref.shape[0]
    head_size = received_ref.shape[2] // 4
    tokens = rows_ref.shape[1] - SLOTS
    factor = head_size ** (-0.5)
    filled = []
    for source in range(sources):
        mark = received_ref[source, :, :head_size].astype(jnp.float32)
        filled.append(jnp.sum((mark < EMPTY).astype(jnp.float32), axis=0, keepdims=True))
    counts_vmem[...] = jnp.concatenate(filled, axis=0).astype(jnp.int32)
    copy = pltpu.make_async_copy(counts_vmem, counts_smem, sem)
    copy.start()
    copy.wait()
    starts = []
    start = 0
    for source in range(sources):
        starts.append(start)
        for part in range(4):
            lanes = slice(part * head_size, (part + 1) * head_size)
            rows_ref[part, pl.ds(start, SLOTS), :] = received_ref[source, :, lanes].astype(
                jnp.float32
            )
        start = jnp.minimum(start + counts_smem[source, 0], tokens)
    block = 256
    key = rows_ref[1, :tokens, :].astype(jnp.bfloat16)
    value = rows_ref[2, :tokens, :].astype(jnp.bfloat16)
    key_grad = jnp.zeros((tokens, head_size), jnp.float32)
    value_grad = jnp.zeros((tokens, head_size), jnp.float32)
    for row in range(0, tokens, block):
        query = rows_ref[0, row : row + block, :].astype(jnp.bfloat16)
        grad = rows_ref[3, row : row + block, :].astype(jnp.bfloat16)
        output, dquery, dscores, weights = softmax_grad(query, key, value, grad, factor, None)
        out_ref[0, row : row + block, :] = output.astype(jnp.float32)
        out_ref[1, row : row + block, :] = dquery.astype(jnp.float32)
        key_grad = key_grad + dot_tn(dscores, query)
        value_grad = value_grad + dot_tn(weights, grad)
    out_ref[2, :tokens, :] = key_grad * factor
    out_ref[3, :tokens, :] = value_grad
    out_ref[:, tokens:, :] = jnp.zeros((4, SLOTS, head_size), jnp.float32)
    stores = []
    for source in range(sources):
        for part in range(4):
            lanes = slice(part * head_size, (part + 1) * head_size)
            result_ref[source, :, lanes] = out_ref[part, pl.ds(starts[source], SLOTS), :].astype(
                jnp.bfloat16
            )
        store = pltpu.make_async_copy(
            result_ref.at[source], result_hbm.at[source], sems.at[source]
        )
        store.start()
        stores.append(store)
    for store in stores:
        store.wait()


def cluster_attention(received, tokens):
    sources, slots, width = received.shape
    vmem = pl.BlockSpec(memory_space=pltpu.VMEM)
    return pl.pallas_call(
        cluster_kernel,
        out_shape=jax.ShapeDtypeStruct(received.shape, jnp.bfloat16),
        in_specs=[vmem],
        out_specs=pl.BlockSpec(memory_space=pl.ANY),
        scratch_shapes=[
            pltpu.VMEM((sources, 128), jnp.int32),
            pltpu.SMEM((sources, 128), jnp.int32),
            pltpu.VMEM((4, tokens + SLOTS, width // 4), jnp.float32),
            pltpu.VMEM((4, tokens + SLOTS, width // 4), jnp.float32),
            pltpu.VMEM(received.shape, jnp.bfloat16),
            pltpu.SemaphoreType.DMA,
            pltpu.SemaphoreType.DMA((sources,)),
        ],
        compiler_params=pltpu.CompilerParams(vmem_limit_bytes=28 << 20),
        name="cluster",
    )(received)


def unroute_kernel(
    returned_ref, target_ref, output_hbm, grads_hbm, output_ref, grads_ref, sems
):
    clusters = returned_ref.shape[0]
    tokens, head_size = output_ref.shape
    slots = clusters * SLOTS
    rows = returned_ref[...].reshape(slots, 4 * head_size)
    block = 256
    lanes = lax.broadcasted_iota(jnp.int32, (block, 128), 1)
    stores = []
    for row in range(0, tokens, block):
        target = target_ref[row : row + block, :]
        select = jnp.concatenate(
            [
                (lanes + lane == target).astype(jnp.float32).astype(jnp.bfloat16)
                for lane in range(0, slots, 128)
            ],
            axis=1,
        )
        picked = dot_nn(select, rows).astype(jnp.bfloat16)
        output_ref[row : row + block, :] = picked[:, :head_size]
        for part in range(3):
            grads_ref[part, row : row + block, :] = picked[
                :, (part + 1) * head_size : (part + 2) * head_size
            ]
        span = pl.ds(row, block)
        step = row // block
        for store in (
            pltpu.make_async_copy(output_ref.at[span], output_hbm.at[span], sems.at[0, step]),
            pltpu.make_async_copy(grads_ref.at[:, span], grads_hbm.at[:, span], sems.at[1, step]),
        ):
            store.start()
            stores.append(store)
    for store in stores:
        store.wait()


def unroute(returned, target, head_size):
    tokens = target.shape[0]
    return pl.pallas_call(
        unroute_kernel,
        out_shape=(
            jax.ShapeDtypeStruct((tokens, head_size), jnp.bfloat16),
            jax.ShapeDtypeStruct((3, tokens, head_size), jnp.bfloat16),
        ),
        in_specs=[pl.BlockSpec(memory_space=pltpu.VMEM)] * 2,
        out_specs=(pl.BlockSpec(memory_space=pl.ANY),) * 2,
        scratch_shapes=[
            pltpu.VMEM((tokens, head_size), jnp.bfloat16),
            pltpu.VMEM((3, tokens, head_size), jnp.bfloat16),
            pltpu.SemaphoreType.DMA((2, 4)),
        ],
        compiler_params=pltpu.CompilerParams(vmem_limit_bytes=20 << 20),
        name="unroute",
    )(returned, target)


def local_kernel(
    index_ref, qkv_ref, grad_ref, prev_ref, output_ref, dquery_ref, own_ref, late_ref, keys, values, key_acc, value_acc
):
    tokens, head_size = grad_ref.shape
    factor = head_size ** (-0.5)
    block = 256
    span = WIN + block
    keys[:tokens, :] = prev_ref[0]
    keys[tokens:, :] = qkv_ref[1]
    values[:tokens, :] = prev_ref[1]
    values[tokens:, :] = qkv_ref[2]
    key_acc[...] = jnp.zeros_like(key_acc)
    value_acc[...] = jnp.zeros_like(value_acc)
    rows = lax.broadcasted_iota(jnp.int32, (block, block), 0)
    columns = lax.broadcasted_iota(jnp.int32, (block, block), 1)
    whole = lax.broadcasted_iota(jnp.int32, (block, span), 1)
    first_key = jnp.where(index_ref[0] == 0, tokens, 0)

    for row in range(0, tokens, block):

        def mask(scores, row=row):
            head = jnp.where(columns > rows, scores[:, :block], masked_fill)
            tail = jnp.where(columns <= rows, scores[:, span - block :], masked_fill)
            joined = jnp.concatenate([head, scores[:, block : span - block], tail], axis=1)
            return jnp.where(whole + row >= first_key, joined, masked_fill)

        query = qkv_ref[0, row : row + block, :]
        grad = grad_ref[row : row + block, :]
        key = keys[row : row + span, :]
        value = values[row : row + span, :]
        output, dquery, dscores, weights = softmax_grad(query, key, value, grad, factor, mask)
        output_ref[row : row + block, :] = output
        dquery_ref[row : row + block, :] = dquery
        key_acc[row : row + span, :] += dot_tn(dscores, query)
        value_acc[row : row + span, :] += dot_tn(weights, grad)
    late_ref[0] = (key_acc[:tokens, :] * factor).astype(jnp.bfloat16)
    late_ref[1] = value_acc[:tokens, :].astype(jnp.bfloat16)
    own_ref[0] = key_acc[tokens:, :] * factor
    own_ref[1] = value_acc[tokens:, :]


def local_attention(index, qkv, grad, prev, cost):
    tokens, head_size = grad.shape
    vmem = pl.BlockSpec(memory_space=pltpu.VMEM)
    return pl.pallas_call(
        local_kernel,
        out_shape=(
            jax.ShapeDtypeStruct((tokens, head_size), jnp.bfloat16),
            jax.ShapeDtypeStruct((tokens, head_size), jnp.bfloat16),
            jax.ShapeDtypeStruct((2, tokens, head_size), jnp.float32),
            jax.ShapeDtypeStruct((2, tokens, head_size), jnp.bfloat16),
        ),
        in_specs=[pl.BlockSpec(memory_space=pltpu.SMEM), vmem, vmem, vmem],
        scratch_shapes=[
            pltpu.VMEM((2 * tokens, head_size), jnp.bfloat16),
            pltpu.VMEM((2 * tokens, head_size), jnp.bfloat16),
            pltpu.VMEM((2 * tokens, head_size), jnp.float32),
            pltpu.VMEM((2 * tokens, head_size), jnp.float32),
        ],
        compiler_params=pltpu.CompilerParams(vmem_limit_bytes=28 << 20),
        cost_estimate=pl.CostEstimate(
            flops=cost, transcendentals=tokens * (WIN + 256), bytes_accessed=12 * tokens * head_size
        ),
        name="local",
    )(index, qkv, grad, prev)


def shifted(block, distance):
    devices = range(lax.axis_size("seq"))
    return lax.ppermute(
        block, "seq", [(i - distance, i) for i in devices if i - distance in devices]
    )


def exchange(block):
    return lax.all_to_all(block, "seq", split_axis=0, concat_axis=0, tiled=True)


def routed_first(local_qkv, local_grad, routed_qkv, routed_grad, cluster_ids):
    tokens, head_size = local_grad.shape
    buffer, target = route(cluster_ids, routed_qkv, routed_grad, lax.axis_size("seq"))
    received = exchange(buffer)
    halo, buffer = lax.optimization_barrier((local_qkv[1:], buffer))
    prev = shifted(halo, 1)
    result = cluster_attention(received, tokens)
    returned = exchange(result)
    index = lax.axis_index("seq").astype(jnp.int32).reshape(1)
    local_out, dquery, own, late = local_attention(
        index, local_qkv, local_grad, prev, HIDDEN_FLOPS
    )
    late = shifted(late, -1)
    joined = (own + late.astype(jnp.float32)).astype(jnp.bfloat16)
    local_dqkv = jnp.concatenate([dquery[None], joined], axis=0)
    routed_out, routed_dqkv = unroute(returned, target, head_size)
    return (local_out, local_dqkv, routed_out, routed_dqkv)


def local_first(local_qkv, local_grad, routed_qkv, routed_grad, cluster_ids):
    tokens, head_size = local_grad.shape
    buffer, target = route(cluster_ids, routed_qkv, routed_grad, lax.axis_size("seq"))
    halo, buffer = lax.optimization_barrier((local_qkv[1:], buffer))
    prev = shifted(halo, 1)
    index = lax.axis_index("seq").astype(jnp.int32).reshape(1)
    local_out, dquery, own, late = local_attention(
        index, local_qkv, local_grad, prev, LOCAL_FLOPS
    )
    buffer, late = lax.optimization_barrier((buffer, late))
    received = exchange(buffer)
    late = shifted(late, -1)
    result = cluster_attention(received, tokens)
    result, late = lax.optimization_barrier((result, late))
    returned = exchange(result)
    joined = (own + late.astype(jnp.float32)).astype(jnp.bfloat16)
    local_dqkv = jnp.concatenate([dquery[None], joined], axis=0)
    routed_out, routed_dqkv = unroute(returned, target, head_size)
    return (local_out, local_dqkv, routed_out, routed_dqkv)


def on_device(*arrays):
    return lax.cond(lax.axis_index("dp") == 0, routed_first, local_first, *arrays)


def solution(mesh):
    rows = P(("dp", "seq"), "head")
    stacked = P(None, ("dp", "seq"), "head")
    return jax.shard_map(
        on_device,
        mesh=mesh,
        in_specs=(stacked, rows, stacked, rows, P("head", ("dp", "seq"))),
        out_specs=(rows, stacked, rows, stacked),
        check_vma=False,
    )
```
